32 devices in a mesh: section: 2 (over y), dp: 8 (over z, x), tensor: 2 (over core).
Axes of the slice: x: 2, y: 2, z: 4, core: 2. Of those that a mesh axis runs over, the one named last changes fastest.
Arguments:
- block_input: bfloat16 [2, 1024, 1024], P(None, 'dp'), may hold values from -6 to 6
- seq_lengths: int32 [2, 8, 4], P(None, 'dp'), may hold values from 1 to 64, 128 in all within a row
- norm_gain: float32 [2, 1024], P('section'), may hold values from 0.5 to 1.5
- in_weight: bfloat16 [2, 1024, 2, 2048], P('section', None, None, 'tensor'), may hold values from -0.1875 to 0.1875
- state_weight: bfloat16 [2, 1024, 256], P('section'), may hold values from -0.1875 to 0.1875
- step_weight: bfloat16 [2, 1024, 32], P('section', None, 'tensor'), may hold values from -0.1875 to 0.1875
- conv_weight: float32 [2, 4, 2048], P('section', None, 'tensor'), may hold values from -3 to 3
- conv_bias: float32 [2, 2048], P('section', 'tensor'), may hold values from -3 to 3
- state_conv: float32 [2, 4, 256], P('section'), may hold values from -3 to 3
- state_bias: float32 [2, 256], P('section'), may hold values from -3 to 3
- step_bias: float32 [2, 32], P('section', 'tensor'), may hold values from -6 to -1
- decay_log: float32 [2, 32], P('section', 'tensor'), may hold values from 0 to 2.77
- skip_gain: float32 [2, 32], P('section', 'tensor'), may hold values from 0.5 to 1.5
- gate_gain: float32 [2, 2048], P('section', 'tensor'), may hold values from 0.5 to 1.5
- out_weight: bfloat16 [2, 2048, 1024], P('section', 'tensor'), may hold values from -0.125 to 0.125
- out_cotangent: bfloat16 [2, 1024, 1024], P(None, 'dp'), may hold values from -6 to 6
Outputs:
- section_output: bfloat16 [2, 2, 1024, 1024], P('section', None, 'dp')
- input_grad: float32 [2, 2, 1024, 1024], P('section', None, 'dp')
- norm_gain_grad: float32 [2, 1024], P('section', 'dp')
- in_weight_grad: float32 [2, 1024, 2, 2048], P('section', 'dp', None, 'tensor')
- state_weight_grad: float32 [2, 1024, 256], P('section', 'dp')
- step_weight_grad: float32 [2, 1024, 32], P('section', 'dp', 'tensor')
- conv_weight_grad: float32 [2, 4, 2048], P('section', None, 'tensor')
- conv_bias_grad: float32 [2, 2048], P('section', 'tensor')
- state_conv_grad: float32 [2, 4, 256], P('section')
- state_bias_grad: float32 [2, 256], P('section')
- step_bias_grad: float32 [2, 32], P('section', 'tensor')
- decay_log_grad: float32 [2, 32], P('section', 'tensor')
- skip_gain_grad: float32 [2, 32], P('section', 'tensor')
- gate_gain_grad: float32 [2, 2048], P('section', 'tensor')
- out_weight_grad: float32 [2, 2048, 1024], P('section', 'tensor', 'dp')
The draws below stay inside these ranges and needn't reach their ends.
Inputs may be any that keep to these rules, and one draw needn't show every extreme that they name: `seq_lengths`: each row of 4 lengths sums to 128, and its longest is exactly 64.
All inputs are finite; a program needn't handle non-finite values.
Results may differ from the reference program's by a relative error of at most 0.018.
The reference program's roundings to bfloat16 on the way (of `normed`, `state_q`, `gated_n`, `grad_q`, `d_ssd_q` and `d_scores_q`) count: a program that leaves them out, or rounds other values in their place, can miss the bound.
Values may be sent and summed in bfloat16 or wider, within the bound.
No kernel may reach another device: no remote copies, remote signals or barrier semaphores. Data moves between devices by JAX's collectives and lax.ppermute only.
A program may use at most 128 MiB of HBM per device.

```python
import math
import jax
import jax.numpy as jnp
import numpy as np
from jax import lax

D = 1024
HEADS = 32
STATE = 128
KERNEL = 4
INNER = 2048
TOK_DEV = 128
MICRO = 2
SEQS = 4
MAXLEN = 64
TOKENS = 1024
N_SECTION = 2
N_DP = 8


def level_of(own_key, extent, pieces, smallest, largest):
    level = 1.0
    for axis_at, blocks in pieces:
        heights = jax.random.uniform(jax.random.fold_in(jax.random.fold_in(own_key, 6), axis_at), (blocks,), jnp.float32, smallest / len(pieces), largest / len(pieces))
        level = level * jnp.repeat(jnp.exp(heights), extent[axis_at] // blocks).reshape((-1,) + (1,) * (len(extent) - 1 - axis_at))
    return level


def profile(number_of, total, bound, skew):
    loads = [(1 << 20) // math.isqrt(rank ** skew) + 1 for rank in range(2, number_of + 1)]
    rest, counts = total - bound - (number_of - 1), [1] * (number_of - 1)
    while rest > 0:
        candidates = [i for i in range(number_of - 1) if counts[i] < bound]
        whole, budget = sum([loads[i] for i in candidates]), rest
        for i in candidates:
            extra = min(bound - counts[i], max(1, budget * loads[i] // whole), rest)
            counts[i] = counts[i] + extra
            rest = rest - extra
    return np.array([bound] + counts)


def uneven_parts(stream_key, number_of, total, bound, lean):
    if number_of == 2:
        one = jax.random.randint(stream_key, (), max(1, total - bound), min(bound, total - 1) + 1)
        return jnp.stack([one, total - one])
    sizes = jnp.asarray(profile(number_of, total, bound, lean), jnp.int32)
    twos = (number_of - 1) // 2
    giver, sink = sizes[1:1 + 2 * twos:2], sizes[2:2 + 2 * twos:2]
    slack = jnp.minimum(giver - 1, bound - sink)
    moved = jax.random.randint(jax.random.fold_in(stream_key, 1), (twos,), 0, 1 << 20) % (slack + 1)
    sizes = sizes.at[1:1 + 2 * twos:2].set(giver - moved).at[2:2 + 2 * twos:2].set(sink + moved)
    return sizes[jax.random.permutation(jax.random.fold_in(stream_key, 2), number_of)]


def scatter_about(key, extent, width, reach, shards=(), kind=jnp.bfloat16):
    array = jax.random.normal(key, extent, jnp.float32) * width
    if len(shards) > 0:
        array = level_of(key, extent, shards, -0.22, 0.18) * array
    return jnp.clip(array, min=-reach, max=reach).astype(kind)


def setup_inputs(seed: int = 0) -> dict:
    arg_keys = jax.random.split(jax.random.key(seed), 17)
    return {
        "block_input": scatter_about(arg_keys[0], (MICRO, TOKENS, D), 1.0, 6.0, ((1, 8),)),
        "seq_lengths": jax.vmap(lambda own: uneven_parts(own, SEQS, TOK_DEV, MAXLEN, 2))(jax.random.split(arg_keys[1], MICRO * N_DP)).reshape((MICRO, N_DP, SEQS)).astype(jnp.int32),
        "norm_gain": jnp.clip(1.0 + 0.1 * jax.random.normal(arg_keys[2], (N_SECTION, D), jnp.float32), 0.5, 1.5),
        "in_weight": scatter_about(arg_keys[3], (N_SECTION, D, 2, INNER), D ** -0.5, 0.1875, ((0, 2), (3, 2))),
        "state_weight": scatter_about(arg_keys[4], (N_SECTION, D, 2 * STATE), D ** -0.5, 0.1875, ((0, 2),)),
        "step_weight": scatter_about(arg_keys[5], (N_SECTION, D, HEADS), D ** -0.5, 0.1875, ((0, 2), (2, 2))),
        "conv_weight": scatter_about(arg_keys[6], (N_SECTION, KERNEL, INNER), 0.5, 3.0, ((0, 2), (2, 2)), jnp.float32),
        "conv_bias": scatter_about(arg_keys[7], (N_SECTION, INNER), 0.5, 3.0, ((0, 2), (1, 2)), jnp.float32),
        "state_conv": scatter_about(arg_keys[8], (N_SECTION, KERNEL, 2 * STATE), 0.5, 3.0, ((0, 2),), jnp.float32),
        "state_bias": scatter_about(arg_keys[9], (N_SECTION, 2 * STATE), 0.5, 3.0, ((0, 2),), jnp.float32),
        "step_bias": jnp.clip(-6.0 + 5.0 * jax.random.uniform(arg_keys[10], (N_SECTION, HEADS), jnp.float32) ** level_of(arg_keys[10], (N_SECTION, HEADS), ((0, 2), (1, 2)), -0.2, 0.2), -6.0, -1.0),
        "decay_log": jnp.clip(2.77 * jax.random.uniform(arg_keys[11], (N_SECTION, HEADS), jnp.float32) ** level_of(arg_keys[11], (N_SECTION, HEADS), ((0, 2), (1, 2)), -0.2, 0.2), 0.0, 2.77),
        "skip_gain": jnp.clip(0.5 + 1.0 * jax.random.uniform(arg_keys[12], (N_SECTION, HEADS), jnp.float32) ** level_of(arg_keys[12], (N_SECTION, HEADS), ((0, 2), (1, 2)), -0.2, 0.2), 0.5, 1.5),
        "gate_gain": jnp.clip(1.0 + 0.1 * jax.random.normal(arg_keys[13], (N_SECTION, INNER), jnp.float32), 0.5, 1.5),
        "out_weight": scatter_about(arg_keys[14], (N_SECTION, INNER, D), INNER ** -0.5, 0.125, ((0, 2), (1, 2))),
        "out_cotangent": scatter_about(arg_keys[15], (MICRO, TOKENS, D), 1.0, 6.0, ((1, 8),)),
    }


EPS = 1e-05

def segment_ids(lengths_row, row_count):
    places = jnp.arange(row_count, dtype=jnp.int32)
    seq_ends = jnp.cumsum(lengths_row.astype(jnp.int32)).astype(jnp.int32)
    return lax.optimization_barrier(jnp.sum((places[:, None] >= seq_ends[None, :]).astype(jnp.int32), axis=1)).astype(jnp.int32)

def norm_piece(residual, norm_scale):
    mean_sq = lax.optimization_barrier(jnp.mean(residual * residual, axis=1, keepdims=True))
    return residual * lax.rsqrt(mean_sq + EPS) * norm_scale[None, :]

def causal_conv(values, weight, bias_row, segment):
    row_count = values.shape[0]
    kernel = weight.shape[0]
    running = bias_row[None, :] + weight[kernel - 1][None, :] * values
    for offset in range(1, kernel):
        shifted = jnp.concatenate([jnp.zeros((offset, values.shape[1]), values.dtype), values[:row_count - offset]], axis=0)
        same_doc = jnp.concatenate([jnp.zeros((offset,), jnp.bool_), segment[offset:] == segment[:row_count - offset]])
        running = running + weight[kernel - 1 - offset][None, :] * jnp.where(same_doc[:, None], shifted, 0.0)
    return jax.nn.silu(running)

def conv_piece(segment):

    def apply_conv(inner_pre, state_pre, conv_weight, conv_bias, state_conv, state_bias):
        return (causal_conv(inner_pre, conv_weight, conv_bias, segment), causal_conv(state_pre, state_conv, state_bias, segment))
    return apply_conv

def mix_piece(segment):

    def apply_mix(step_raw, step_bias, decay_log, scores):
        row_count = step_raw.shape[0]
        step_size = jax.nn.softplus(step_raw + step_bias[None, :])
        decay_rate = -jnp.exp(decay_log)
        cumulated = jnp.cumsum(step_size * decay_rate[None, :], axis=0)
        places = jnp.arange(row_count, dtype=jnp.int32)
        allowed = (places[:, None] >= places[None, :]) & (segment[:, None] == segment[None, :])
        spread = cumulated.T[:, :, None] - cumulated.T[:, None, :]
        decay_mat = jnp.exp(jnp.where(allowed[None], spread, -1e+30))
        return scores[None] * decay_mat * step_size.T[:, None, :]
    return apply_mix

def forward_layer(hidden, segment, params):
    norm_gain, in_weight, state_weight, step_weight, conv_weight, conv_bias, state_conv, state_bias, step_bias, decay_log, skip_gain, gate_gain, out_weight = params
    row_count = hidden.shape[0]
    inner_width = in_weight.shape[2]
    head_count = step_weight.shape[1]
    residual = hidden.astype(jnp.float32)
    normed = norm_piece(residual, norm_gain).astype(jnp.bfloat16)
    both_cols = jnp.dot(normed, in_weight.reshape(in_weight.shape[0], 2 * inner_width), preferred_element_type=jnp.float32)
    gate_pre = both_cols[:, :inner_width]
    inner_pre = both_cols[:, inner_width:]
    state_pre = jnp.dot(normed, state_weight, preferred_element_type=jnp.float32)
    step_raw = jnp.dot(normed, step_weight, preferred_element_type=jnp.float32)
    inner_act, state_act = conv_piece(segment)(inner_pre, state_pre, conv_weight, conv_bias, state_conv, state_bias)
    state_q = state_act.astype(jnp.bfloat16)
    half_width = state_q.shape[1] // 2
    scores = jnp.dot(state_q[:, half_width:], state_q[:, :half_width].T, preferred_element_type=jnp.float32)
    mixing = mix_piece(segment)(step_raw, step_bias, decay_log, scores)
    mixing_q = mixing.astype(jnp.bfloat16)
    inner_q = inner_act.astype(jnp.bfloat16).reshape(row_count, head_count, -1)
    mixed_out = jnp.einsum('hts,shp->thp', mixing_q.astype(jnp.float32), inner_q.astype(jnp.float32))
    ssd_out = (mixed_out + skip_gain[None, :, None] * inner_act.reshape(row_count, head_count, -1)).reshape(row_count, inner_width)
    gate_sig = jax.nn.sigmoid(gate_pre)
    gated_raw = ssd_out * gate_pre * gate_sig
    inverse = lax.rsqrt(lax.optimization_barrier(jnp.mean(gated_raw * gated_raw, axis=1, keepdims=True)) + EPS)
    gated_n = (gated_raw * inverse * gate_gain[None, :]).astype(jnp.bfloat16)
    out_part = jnp.dot(gated_n, out_weight, preferred_element_type=jnp.float32)
    new_hidden = (residual + out_part).astype(jnp.bfloat16)
    kept_state = (residual, normed, gate_pre, inner_pre, state_pre, step_raw, inner_act, state_q, scores, mixing_q, inner_q, ssd_out, gate_sig, gated_raw, inverse, gated_n)
    return (new_hidden, kept_state)

def backward_layer(grad_out, kept_state, segment, params):
    norm_gain, in_weight, state_weight, step_weight, conv_weight, conv_bias, state_conv, state_bias, step_bias, decay_log, skip_gain, gate_gain, out_weight = params
    residual, normed, gate_pre, inner_pre, state_pre, step_raw, inner_act, state_q, scores, mixing_q, inner_q, ssd_out, gate_sig, gated_raw, inverse, gated_n = kept_state
    row_count = grad_out.shape[0]
    inner_width = in_weight.shape[2]
    head_count = step_weight.shape[1]
    grad_q = grad_out.astype(jnp.bfloat16)
    d_out_weight = jnp.dot(gated_n.T, grad_q, preferred_element_type=jnp.float32)
    d_gated_n = jnp.dot(grad_q, out_weight.T, preferred_element_type=jnp.float32)
    d_gate_gain = lax.optimization_barrier(jnp.sum(d_gated_n * gated_raw * inverse, axis=0))
    inner_total = lax.optimization_barrier(jnp.sum(d_gated_n * gate_gain[None, :] * gated_raw, axis=1, keepdims=True))
    d_gated = inverse * gate_gain[None, :] * d_gated_n - gated_raw * inverse * inverse * inverse * inner_total / inner_width
    d_ssd = d_gated * gate_pre * gate_sig
    d_gate_pre = d_gated * ssd_out * gate_sig * (1.0 + gate_pre * (1.0 - gate_sig))
    d_ssd_heads = d_ssd.reshape(row_count, head_count, -1)
    d_ssd_q = d_ssd_heads.astype(jnp.bfloat16)
    d_skip = lax.optimization_barrier(jnp.sum(d_ssd_heads * inner_act.reshape(row_count, head_count, -1), axis=(0, 2)))
    d_mixing = jnp.einsum('thp,shp->hts', d_ssd_q.astype(jnp.float32), inner_q.astype(jnp.float32))
    d_inner = (jnp.einsum('hts,thp->shp', mixing_q.astype(jnp.float32), d_ssd_q.astype(jnp.float32)) + skip_gain[None, :, None] * d_ssd_heads).reshape(row_count, inner_width)
    mix_value, mix_back = jax.vjp(mix_piece(segment), step_raw, step_bias, decay_log, scores)
    d_step_raw, d_step_bias, d_decay_log, d_scores = mix_back(d_mixing)
    d_scores_q = d_scores.astype(jnp.bfloat16)
    half_width = state_q.shape[1] // 2
    d_out_state = jnp.dot(d_scores_q, state_q[:, :half_width], preferred_element_type=jnp.float32)
    d_in_state = jnp.dot(d_scores_q.T, state_q[:, half_width:], preferred_element_type=jnp.float32)
    d_state_act = jnp.concatenate([d_in_state, d_out_state], axis=1)
    conv_value, conv_back = jax.vjp(conv_piece(segment), inner_pre, state_pre, conv_weight, conv_bias, state_conv, state_bias)
    d_inner_pre, d_state_pre, d_conv_weight, d_conv_bias, d_state_conv, d_state_bias = conv_back((d_inner, d_state_act))
    d_both_q = jnp.concatenate([d_gate_pre, d_inner_pre], axis=1).astype(jnp.bfloat16)
    d_state_q = d_state_pre.astype(jnp.bfloat16)
    d_step_q = d_step_raw.astype(jnp.bfloat16)
    in_flat = in_weight.reshape(in_weight.shape[0], 2 * inner_width)
    d_normed = jnp.dot(d_both_q, in_flat.T, preferred_element_type=jnp.float32) + jnp.dot(d_step_q, step_weight.T, preferred_element_type=jnp.float32) + jnp.dot(d_state_q, state_weight.T, preferred_element_type=jnp.float32)
    d_in_weight = jnp.dot(normed.T, d_both_q, preferred_element_type=jnp.float32).reshape(in_weight.shape)
    d_state_weight = jnp.dot(normed.T, d_state_q, preferred_element_type=jnp.float32)
    d_step_weight = jnp.dot(normed.T, d_step_q, preferred_element_type=jnp.float32)
    norm_value, norm_back = jax.vjp(norm_piece, residual, norm_gain)
    d_residual, d_norm_gain = norm_back(d_normed)
    input_grad = grad_out + d_residual
    grads = (d_norm_gain, d_in_weight, d_state_weight, d_step_weight, d_conv_weight, d_conv_bias, d_state_conv, d_state_bias, d_step_bias, d_decay_log, d_skip, d_gate_gain, d_out_weight)
    return (input_grad, grads)

def reference(block_input, seq_lengths, norm_gain, in_weight, state_weight, step_weight, conv_weight, conv_bias, state_conv, state_bias, step_bias, decay_log, skip_gain, gate_gain, out_weight, out_cotangent):
    weights = (norm_gain, in_weight, state_weight, step_weight, conv_weight, conv_bias, state_conv, state_bias, step_bias, decay_log, skip_gain, gate_gain, out_weight)
    first_params = tuple((weight[0] for weight in weights))
    second_params = tuple((weight[1] for weight in weights))
    row_total = MICRO * N_DP
    inputs = block_input.reshape(row_total, TOK_DEV, D)
    cotangents = out_cotangent.reshape(row_total, TOK_DEV, D)
    lengths = seq_lengths.reshape(row_total, SEQS)
    zero_grads = tuple((jnp.zeros(weight.shape[1:], jnp.float32) for weight in weights))

    def visit_row(grads_in, row_data):
        hidden, cotangent, lengths_row = row_data
        segment = segment_ids(lengths_row, TOK_DEV)
        middle, kept_first = forward_layer(hidden, segment, first_params)
        final_out, kept_second = forward_layer(middle, segment, second_params)
        grad_middle, grads_second = backward_layer(cotangent.astype(jnp.float32), kept_second, segment, second_params)
        grad_input, grads_first = backward_layer(grad_middle, kept_first, segment, first_params)
        new_first = jax.tree.map(jnp.add, grads_in[0], grads_first)
        new_second = jax.tree.map(jnp.add, grads_in[1], grads_second)
        return ((new_first, new_second), (middle, final_out, grad_middle, grad_input))
    totals, outputs = lax.scan(visit_row, (zero_grads, zero_grads), (inputs, cotangents, lengths))
    middle, final_out, grad_middle, grad_input = outputs
    section_output = jnp.stack([middle.reshape(MICRO, TOKENS, D), final_out.reshape(MICRO, TOKENS, D)])
    input_grad = jnp.stack([grad_input.reshape(MICRO, TOKENS, D), grad_middle.reshape(MICRO, TOKENS, D)])
    stacked = tuple((jnp.stack([first_grad, second_grad]) for first_grad, second_grad in zip(totals[0], totals[1])))
    return (section_output, input_grad, stacked[0], stacked[1], stacked[2], stacked[3], stacked[4], stacked[5], stacked[6], stacked[7], stacked[8], stacked[9], stacked[10], stacked[11], stacked[12])
```

```python
import functools

import jax
import jax.numpy as jnp
from jax import lax
from jax.experimental import pallas as pl
from jax.experimental.pallas import tpu as pltpu
from jax.sharding import PartitionSpec as P

EPS = 1e-05
LANES = 128
BLOCK = 256
NT = (((1,), (1,)), ((), ()))
TN = (((0,), (0,)), ((), ()))
F32 = jnp.float32
BF16 = jnp.bfloat16


def matmul(left, right):
    return jnp.dot(left, right, preferred_element_type=F32)


def matmul_nt(left, right):
    return lax.dot_general(left, right, NT, preferred_element_type=F32)


def matmul_tn(left, right):
    return lax.dot_general(left, right, TN, preferred_element_type=F32)


def down(values, steps):
    return pltpu.roll(values, steps, 0)


def up(values, steps):
    return pltpu.roll(values, values.shape[0] - steps, 0)


def col_sum(values):
    return jnp.sum(values, axis=0, keepdims=True)


def fold(values):
    total = values[:, :LANES]
    for start in range(LANES, values.shape[1], LANES):
        total = total + values[:, start : start + LANES]
    return total


class Row:
    def __init__(self, lengths_ref, rows):
        wide = (rows, BLOCK)
        place = lax.broadcasted_iota(jnp.int32, wide, 0)
        lane = lax.broadcasted_iota(jnp.int32, (rows, rows), 1)
        segment = jnp.zeros(wide, jnp.int32)
        segment_lane = jnp.zeros((rows, rows), jnp.int32)
        end = jnp.int32(0)
        for number in range(lengths_ref.shape[1]):
            end = end + lengths_ref[0, number]
            segment = segment + jnp.where(place >= end, 1, 0)
            segment_lane = segment_lane + jnp.where(lane >= end, 1, 0)
        self.rows = rows
        self.allowed = (place[:, :rows] >= lane) & (segment[:, :rows] == segment_lane)
        self.place = place[:, :LANES]
        self.same = [None]
        for steps in range(1, 4):
            kept = (place >= steps) & (segment == down(segment, steps))
            self.same.append(jnp.where(kept, 1.0, 0.0).astype(F32))


def conv_pre(row, values, taps, bias):
    kernel = len(taps)
    running = bias + taps[kernel - 1] * values
    for steps in range(1, kernel):
        running = running + taps[kernel - 1 - steps] * (row.same[steps] * down(values, steps))
    return running


def conv_back(row, d_pre, values, taps):
    kernel = len(taps)
    d_values = taps[kernel - 1] * d_pre
    d_taps = [None] * kernel
    d_taps[kernel - 1] = col_sum(d_pre * values)
    for steps in range(1, kernel):
        masked = row.same[steps] * d_pre
        d_values = d_values + taps[kernel - 1 - steps] * up(masked, steps)
        d_taps[kernel - 1 - steps] = col_sum(masked * down(values, steps))
    return d_values, d_taps, col_sum(d_pre)


def silu_back(pre, sig):
    return sig * (1.0 + pre * (1.0 - sig))


def softplus(values):
    return jnp.maximum(values, 0.0) + jnp.log1p(jnp.exp(-jnp.abs(values)))


def running_sum(row, values):
    steps = 1
    while steps < row.rows:
        values = values + jnp.where(row.place >= steps, down(values, steps), 0.0)
        steps *= 2
    return values


def running_sum_back(row, values):
    steps = 1
    while steps < row.rows:
        values = values + jnp.where(row.place < row.rows - steps, up(values, steps), 0.0)
        steps *= 2
    return values


def block_at(index):
    return pl.ds(pl.multiple_of(index * BLOCK, BLOCK), BLOCK)


def split_heads(values, low):
    return jnp.concatenate(
        [jnp.where(low, values, 0.0), jnp.where(low, 0.0, values)], axis=0
    ).astype(BF16)


def tap_rows(ref, where):
    return [ref[number : number + 1, where] for number in range(4)]


def mixer_inputs(row, keep, par):
    state_pre = keep["state_pre"][...]
    taps = [par["state"][number : number + 1, :] for number in range(4)]
    pre = conv_pre(row, state_pre, taps, par["state"][4:5, :])
    sig = jax.nn.sigmoid(pre)
    state_q = (pre * sig).astype(BF16)
    half = state_q.shape[1] // 2
    in_state, out_state = state_q[:, :half], state_q[:, half:]
    scores = matmul_nt(out_state, in_state)
    step_in = keep["step_raw"][...] + par["head"][0:1, :]
    step = softplus(step_in)
    rate = -jnp.exp(par["head"][1:2, :])
    cumulated = running_sum(row, step * rate)
    keep["step_t"][...] = step.T
    keep["cum_t"][...] = cumulated.T
    return dict(
        pre=pre,
        sig=sig,
        taps=taps,
        state_pre=state_pre,
        in_state=in_state,
        out_state=out_state,
        scores=scores,
        step_in=step_in,
        step=step,
        rate=rate,
        cumulated=cumulated,
    )


def decay_of(row, rolled, keep, first, number):
    head = first + number
    spread = rolled[:, number : number + 1] - keep["cum_t"][pl.ds(head, 1), :]
    decay = jnp.exp(jnp.where(row.allowed, spread, -1e30))
    return head, decay, keep["step_t"][pl.ds(head, 1), :]


def norm_parts(x_ref, par):
    residual = x_ref[...].astype(F32)
    width = residual.shape[1]
    inverse = lax.rsqrt(jnp.sum(residual * residual, axis=1, keepdims=True) / width + EPS)
    return residual, inverse, (residual * inverse * par["norm"][...]).astype(BF16)


def forward(row, x_ref, par, keep, weights, out_ref):
    rows = row.rows
    inner = keep["gate"].shape[1]
    local = inner // 2
    head_dim = LANES // 2
    per_block = BLOCK // head_dim
    half_blocks = local // BLOCK
    residual, inverse_norm, normed = norm_parts(x_ref, par)
    keep["normed"][...] = normed
    weights.wait("state")
    keep["state_pre"][...] = matmul(normed, weights.state[...])
    keep["step_raw"][...] = matmul(normed, weights.step[...])
    mixer = mixer_inputs(row, keep, par)
    scores, cumulated = mixer["scores"], mixer["cumulated"]
    low = lax.broadcasted_iota(jnp.int32, (rows, LANES), 1) < head_dim

    def body(index, squares):
        where = block_at(index)
        half = index // half_blocks
        start = half * (2 * half_blocks) + (index - half * half_blocks)
        gate = matmul(keep["normed"][...], weights.inward[:, block_at(start)])
        value = matmul(keep["normed"][...], weights.inward[:, block_at(start + half_blocks)])
        keep["gate"][:, where] = gate
        keep["inner"][:, where] = value
        pre = conv_pre(row, value, tap_rows(par["inner"], where), par["inner"][4:5, where])
        act = pre * jax.nn.sigmoid(pre)
        first = index * per_block
        rolled = pltpu.roll(cumulated, LANES - first, 1)
        outs = []
        for pair in range(per_block // 2):
            mixes = []
            for number in (2 * pair, 2 * pair + 1):
                _, decay, step_row = decay_of(row, rolled, keep, first, number)
                mixes.append((scores * decay * step_row).astype(BF16))
            values = split_heads(act[:, pair * LANES : (pair + 1) * LANES], low)
            outs.append(matmul(jnp.concatenate(mixes, axis=1), values))
        ssd = jnp.concatenate(outs, axis=1) + par["inner"][6:7, where] * act
        keep["ssd"][:, where] = ssd
        raw = ssd * gate * jax.nn.sigmoid(gate)
        return squares + fold(raw * raw)

    weights.wait("own")
    squares = lax.fori_loop(0, half_blocks, body, jnp.zeros((rows, LANES), F32))
    weights.wait("other")
    squares = lax.fori_loop(half_blocks, 2 * half_blocks, body, squares)
    inverse = lax.rsqrt(jnp.sum(squares, axis=1, keepdims=True) / inner + EPS)
    keep["inverse"][...] = jnp.broadcast_to(inverse, (rows, LANES))

    def normalize(index, carry):
        where = block_at(index)
        gate = keep["gate"][:, where]
        raw = keep["ssd"][:, where] * gate * jax.nn.sigmoid(gate)
        keep["gated_n"][:, where] = (raw * inverse * par["inner"][5:6, where]).astype(BF16)
        return carry

    lax.fori_loop(0, inner // BLOCK, normalize, 0)
    weights.wait("out")

    def project(index, carry):
        where = block_at(index)
        total = matmul(keep["gated_n"][...], weights.outward[:, where])
        out_ref[:, where] = (x_ref[:, where].astype(F32) + total).astype(BF16)
        return carry

    lax.fori_loop(0, out_ref.shape[1] // BLOCK, project, 0)


def backward(row, x_ref, grad_ref, par, keep, weights, out, full):
    rows = row.rows
    inner = keep["gate"].shape[1]
    local = inner // 2
    head_dim = LANES // 2
    per_block = BLOCK // head_dim
    half_blocks = local // BLOCK
    blocks = inner // BLOCK
    inverse = keep["inverse"][:, 0:1]
    weights.wait("out")

    def spread_grad(index, total):
        where = block_at(index)
        gate = keep["gate"][:, where]
        raw = keep["ssd"][:, where] * gate * jax.nn.sigmoid(gate)
        d_gated_n = matmul_nt(grad_ref[...], weights.outward[where, :])
        keep["d_gated_n"][:, where] = d_gated_n
        if full:
            half = index // half_blocks
            local_where = block_at(index - half * half_blocks)
            out["inner_grad"][half, 5:6, local_where] = col_sum(d_gated_n * raw * inverse)
        return total + fold(d_gated_n * par["inner"][5:6, where] * raw)

    total = lax.fori_loop(0, blocks, spread_grad, jnp.zeros((rows, LANES), F32))
    inner_total = jnp.sum(total, axis=1, keepdims=True)
    pull = inverse * inverse * inverse * inner_total / inner
    mixer = mixer_inputs(row, keep, par)
    scores, cumulated = mixer["scores"], mixer["cumulated"]
    lane = lax.broadcasted_iota(jnp.int32, (rows, LANES), 1)
    low = lane < head_dim

    def body(index, carry):
        d_scores, row_sums = carry
        where = block_at(index)
        half = index // half_blocks
        within = index - half * half_blocks
        local_where = block_at(within)
        gate = keep["gate"][:, where]
        ssd = keep["ssd"][:, where]
        sig = jax.nn.sigmoid(gate)
        act_gate = gate * sig
        d_gated = (
            inverse * par["inner"][5:6, where] * keep["d_gated_n"][:, where]
            - ssd * act_gate * pull
        )
        d_ssd = d_gated * act_gate
        d_gate = d_gated * ssd * silu_back(gate, sig)
        value = keep["inner"][:, where]
        taps = tap_rows(par["inner"], where)
        pre = conv_pre(row, value, taps, par["inner"][4:5, where])
        pre_sig = jax.nn.sigmoid(pre)
        act = pre * pre_sig
        first = index * per_block
        rolled = pltpu.roll(cumulated, LANES - first, 1)
        d_inner = []
        for pair in range(per_block // 2):
            lanes = slice(pair * LANES, (pair + 1) * LANES)
            values = split_heads(act[:, lanes], low)
            d_pair = d_ssd[:, lanes]
            d_mix = matmul_nt(d_pair.astype(BF16), values)
            mixes = []
            for place in range(2):
                head, decay, step_row = decay_of(row, rolled, keep, first, 2 * pair + place)
                part = d_mix[:, place * rows : (place + 1) * rows] * decay
                weighted = part * step_row
                d_scores = d_scores + weighted
                keep["d_col"][pl.ds(head, 1), :] = col_sum(part * scores)
                row_sum = jnp.sum(weighted * scores, axis=1, keepdims=True)
                row_sums = jnp.where(lane == head, row_sum, row_sums)
                mixes.append((scores * decay * step_row).astype(BF16))
            d_inner.append(matmul_tn(jnp.concatenate(mixes, axis=0), split_heads(d_pair, low)))
        d_act = jnp.concatenate(d_inner, axis=1) + par["inner"][6:7, where] * d_ssd
        d_value, d_taps, d_bias = conv_back(row, d_act * silu_back(pre, pre_sig), value, taps)
        keep["d_both"][half, :, local_where] = d_gate.astype(BF16)
        keep["d_both"][half, :, block_at(within + half_blocks)] = d_value.astype(BF16)
        if full:
            for number in range(4):
                out["inner_grad"][half, number : number + 1, local_where] = d_taps[number]
            out["inner_grad"][half, 4:5, local_where] = d_bias
            out["inner_grad"][half, 6:7, local_where] = col_sum(d_ssd * act)
        return d_scores, row_sums

    zero = jnp.zeros((rows, LANES), F32)
    keep["d_col"][...] = jnp.zeros(keep["d_col"].shape, F32)
    d_scores, row_sums = lax.fori_loop(0, blocks, body, (zero, zero))
    d_col = keep["d_col"][...]
    d_cumulated = row_sums - (d_col * keep["step_t"][...]).T
    d_scaled = running_sum_back(row, d_cumulated)
    d_step = d_col.T + d_scaled * mixer["rate"]
    d_step_raw = d_step * jax.nn.sigmoid(mixer["step_in"])
    d_step_q = d_step_raw.astype(BF16)
    d_scores_q = d_scores.astype(BF16)
    d_state_act = jnp.concatenate(
        [
            matmul_tn(d_scores_q, mixer["out_state"]),
            matmul(d_scores_q, mixer["in_state"]),
        ],
        axis=1,
    )
    d_state, d_taps, d_bias = conv_back(
        row,
        d_state_act * silu_back(mixer["pre"], mixer["sig"]),
        mixer["state_pre"],
        mixer["taps"],
    )
    d_state_q = d_state.astype(BF16)
    weights.wait("state")
    weights.wait("own")
    weights.wait("other")
    residual, inverse_norm, _ = norm_parts(x_ref, par)
    keep["d_normed"][...] = matmul_nt(d_step_q, weights.step[...]) + matmul_nt(
        d_state_q, weights.state[...]
    )
    width = residual.shape[1]

    def project(index, carry):
        where = block_at(index)
        total = keep["d_normed"][:, where]
        for half in range(2):
            span = slice(half * inner, (half + 1) * inner)
            total = total + matmul_nt(keep["d_both"][half], weights.inward[where, span])
        keep["d_normed"][:, where] = total
        return carry

    lax.fori_loop(0, width // BLOCK, project, 0)
    d_normed = keep["d_normed"][...]
    scaled = d_normed * par["norm"][...]
    mean = jnp.sum(scaled * residual, axis=1, keepdims=True) / width
    d_residual = inverse_norm * scaled - residual * (
        inverse_norm * inverse_norm * inverse_norm * mean
    )
    input_grad = grad_ref[...].astype(F32) + d_residual
    if not full:
        out["grad"][...] = input_grad.astype(BF16)
        return
    out["grad"][...] = input_grad
    out["norm_grad"][...] = col_sum(d_normed * residual * inverse_norm)
    out["d_state"][...] = d_state_q
    out["d_step"][...] = d_step_q
    for number in range(4):
        out["state_grad"][number : number + 1, :] = d_taps[number]
    out["state_grad"][4:5, :] = d_bias
    out["state_grad"][5:8, :] = jnp.zeros((3, d_bias.shape[1]), F32)
    head_grad = jnp.concatenate(
        [
            col_sum(d_step_raw),
            col_sum(d_scaled * mixer["step"]) * mixer["rate"],
            jnp.zeros((6, LANES), F32),
        ],
        axis=0,
    )
    out["head_grad"][...] = head_grad
    for half in range(2):
        out["inner_grad"][half, 7:8, :] = jnp.zeros((1, local), F32)


class Weights:
    def __init__(self, sources, scratch, sems):
        own_in, other_in, own_out, other_out, state, step = sources
        self.inward, self.outward, self.state, self.step = scratch
        inner = own_in.shape[1]
        rows = own_out.shape[0]
        self.copies = {
            "state": [(state, self.state), (step, self.step)],
            "own": [(own_in, self.inward.at[:, pl.ds(0, inner)])],
            "other": [(other_in, self.inward.at[:, pl.ds(inner, inner)])],
            "out": [
                (own_out, self.outward.at[pl.ds(0, rows), :]),
                (other_out, self.outward.at[pl.ds(rows, rows), :]),
            ],
        }
        self.sems = sems
        self.made = {}
        self.waited = set()

    def start(self, order):
        number = 0
        for name in order:
            for source, target in self.copies[name]:
                copy = pltpu.make_async_copy(source, target, self.sems.at[number])
                copy.start()
                self.made.setdefault(name, []).append(copy)
                number += 1

    def wait(self, name):
        if name in self.waited:
            return
        self.waited.add(name)
        for copy in self.made[name]:
            copy.wait()


KEPT = ("normed", "gate", "inner", "ssd", "state_pre", "step_raw", "inverse", "gated_n")
FULL_OUT = ("grad", "d_both", "inner_grad", "norm_grad", "d_state", "d_step", "state_grad", "head_grad")


def kernel_body(mode, names, *refs):
    refs = dict(zip(names, refs))
    par = dict(
        norm=refs["norm_par"],
        inner=refs["inner_par"],
        state=refs["state_par"],
        head=refs["head_par"],
    )
    weights = Weights(
        [refs[name] for name in WEIGHTS],
        [refs[name] for name in ("w_in", "w_out", "w_state", "w_step")],
        refs["sems"],
    )
    if mode == "back":
        weights.start(("out", "state", "own", "other"))
    else:
        weights.start(("state", "own", "other", "out"))
    row = Row(refs["lengths"], refs["x"].shape[0])
    if mode != "back":
        forward(row, refs["x"], par, refs, weights, refs["result"])
    if mode != "forward":
        backward(row, refs["x"], refs["grad_in"], par, refs, weights, refs, mode == "back")


WEIGHTS = ("own_in", "other_in", "own_out", "other_out", "state_w", "step_w")


def layer_kernel(mode, args):
    rows, width = args["x"].shape
    inner = args["inner_par"].shape[1]
    state = args["state_w"].shape[1]
    shapes = dict(
        normed=((rows, width), BF16),
        gate=((rows, inner), F32),
        inner=((rows, inner), F32),
        ssd=((rows, inner), F32),
        state_pre=((rows, state), F32),
        step_raw=((rows, LANES), F32),
        inverse=((rows, LANES), F32),
        gated_n=((rows, inner), BF16),
        result=((rows, width), BF16),
        grad=((rows, width), F32 if mode == "back" else BF16),
        d_both=((2, rows, inner), BF16),
        inner_grad=((2, 8, inner // 2), F32),
        norm_grad=((1, width), F32),
        d_state=((rows, state), BF16),
        d_step=((rows, LANES), BF16),
        state_grad=((8, state), F32),
        head_grad=((8, LANES), F32),
        step_t=((LANES, rows), F32),
        cum_t=((LANES, rows), F32),
        d_col=((LANES, rows), F32),
        d_gated_n=((rows, inner), F32),
        d_normed=((rows, width), F32),
        w_in=((width, 2 * inner), BF16),
        w_out=((inner, width), BF16),
        w_state=((width, state), BF16),
        w_step=((width, LANES), BF16),
    )
    inputs = ["x", "lengths", "norm_par", "inner_par", "state_par", "head_par", *WEIGHTS]
    if mode == "forward":
        outputs = ["result"]
        scratch = [*KEPT, "step_t", "cum_t"]
    elif mode == "both":
        inputs += ["grad_in"]
        outputs = ["result", *KEPT, "grad"]
        scratch = ["step_t", "cum_t", "d_both", "d_col", "d_gated_n", "d_normed"]
    else:
        inputs += ["grad_in", *KEPT[1:7]]
        outputs = list(FULL_OUT)
        scratch = ["step_t", "cum_t", "d_col", "d_gated_n", "d_normed"]
    scratch += ["w_in", "w_out", "w_state", "w_step"]
    vmem = pl.BlockSpec(memory_space=pltpu.VMEM)

    def spec(name):
        if name in WEIGHTS:
            return pl.BlockSpec(memory_space=pl.ANY)
        if name == "lengths":
            return pl.BlockSpec(memory_space=pltpu.SMEM)
        return vmem

    names = inputs + outputs + scratch + ["sems"]
    results = pl.pallas_call(
        functools.partial(kernel_body, mode, names),
        name="layer_" + mode,
        out_shape=[jax.ShapeDtypeStruct(*shapes[name]) for name in outputs],
        in_specs=[spec(name) for name in inputs],
        out_specs=[vmem for _ in outputs],
        scratch_shapes=[pltpu.VMEM(*shapes[name]) for name in scratch]
        + [pltpu.SemaphoreType.DMA((len(WEIGHTS),))],
        compiler_params=pltpu.CompilerParams(vmem_limit_bytes=56 << 20),
        cost_estimate=pl.CostEstimate(
            flops=2 * rows * width * 3 * inner * (1 if mode == "forward" else 2),
            bytes_accessed=2 * width * 3 * inner,
            transcendentals=rows * rows * inner // 64,
        ),
    )(*[args[name] for name in inputs])
    return dict(zip(outputs, results))


def swap(value):
    return lax.ppermute(value, "tensor", [(0, 1), (1, 0)])


def to_section(value, source, target):
    return lax.ppermute(value, "section", [(source, target)])


def in_order(own, other, first):
    return jnp.where(first, jnp.stack([own, other]), jnp.stack([other, own]))


def local(
    block_input,
    seq_lengths,
    norm_gain,
    in_weight,
    state_weight,
    step_weight,
    conv_weight,
    conv_bias,
    state_conv,
    state_bias,
    step_bias,
    decay_log,
    skip_gain,
    gate_gain,
    out_weight,
    out_cotangent,
):
    core = lax.axis_index("tensor")
    first_core = core == 0
    first_section = lax.axis_index("section") == 0
    width, _, half = in_weight.shape[1:]
    heads = step_weight.shape[2]
    head_dim = half // heads
    own_in = in_weight[0].reshape(width, 2 * half)
    other_in = swap(own_in)
    own_out = out_weight[0]
    other_out = swap(own_out)
    own_step = step_weight[0]
    other_step = swap(own_step)
    own_par = jnp.concatenate(
        [
            conv_weight[0],
            conv_bias,
            gate_gain,
            jnp.repeat(skip_gain, head_dim, axis=1),
            jnp.concatenate(
                [step_bias, decay_log, jnp.zeros((1, half - 2 * heads), F32)], axis=1
            ),
        ],
        axis=0,
    )
    other_par = swap(own_par)

    def pad_lanes(value, lanes):
        return jnp.pad(value, ((0, 0), (0, lanes - value.shape[1])))

    args = dict(
        lengths=lax.dynamic_slice_in_dim(seq_lengths[:, 0], core, 1, axis=0),
        norm_par=norm_gain,
        inner_par=jnp.concatenate([own_par, other_par], axis=1),
        state_par=jnp.concatenate(
            [state_conv[0], state_bias, jnp.zeros((3, state_bias.shape[1]), F32)], axis=0
        ),
        head_par=jnp.concatenate(
            [
                pad_lanes(jnp.concatenate([own_par[7:8, :heads], other_par[7:8, :heads]], 1), LANES),
                pad_lanes(
                    jnp.concatenate(
                        [own_par[7:8, heads : 2 * heads], other_par[7:8, heads : 2 * heads]], 1
                    ),
                    LANES,
                ),
                jnp.zeros((6, LANES), F32),
            ],
            axis=0,
        ),
        own_in=own_in,
        other_in=other_in,
        own_out=own_out,
        other_out=other_out,
        state_w=state_weight[0],
        step_w=pad_lanes(jnp.concatenate([own_step, other_step], axis=1), LANES),
    )
    first_input = lax.dynamic_index_in_dim(block_input, core, 0, keepdims=False)
    cotangent = lax.dynamic_index_in_dim(out_cotangent, core, 0, keepdims=False)

    middle = layer_kernel("forward", dict(args, x=first_input))["result"]
    carried = to_section(middle, 0, 1)
    hidden = jnp.where(first_section, first_input, carried)
    kept = layer_kernel("both", dict(args, x=hidden, grad_in=cotangent))
    grad_carried = to_section(kept["grad"], 1, 0)
    grad_in = jnp.where(first_section, grad_carried, cotangent)
    back = layer_kernel("back", dict(args, x=hidden, grad_in=grad_in, **{k: kept[k] for k in KEPT[1:7]}))

    section_output = in_order(kept["result"], swap(kept["result"]), first_core)
    input_grad = in_order(back["grad"], swap(back["grad"]), first_core)

    def both_rows(own, other):
        return jnp.concatenate([own, other], axis=0)

    normed = both_rows(kept["normed"], swap(kept["normed"]))
    gated_n = both_rows(kept["gated_n"][:, :half], swap(kept["gated_n"][:, half:]))
    grad_q = both_rows(grad_in, swap(grad_in))
    d_both = both_rows(back["d_both"][0], swap(back["d_both"][1]))
    state = back["d_state"].shape[1]
    d_state_own = lax.dynamic_slice_in_dim(back["d_state"], core * (state // 2), state // 2, 1)
    d_state_other = lax.dynamic_slice_in_dim(
        back["d_state"], (1 - core) * (state // 2), state // 2, 1
    )
    small_q = both_rows(
        jnp.concatenate([d_state_own, back["d_step"][:, :heads]], axis=1),
        swap(jnp.concatenate([d_state_other, back["d_step"][:, heads : 2 * heads]], axis=1)),
    )
    out_sum = lax.psum_scatter(
        matmul_tn(grad_q, gated_n).astype(BF16), "dp", scatter_dimension=0, tiled=True
    )
    in_sum = lax.psum_scatter(
        matmul_tn(normed, d_both).astype(BF16), "dp", scatter_dimension=0, tiled=True
    )
    small_sum = lax.psum_scatter(
        matmul_tn(normed, small_q).astype(BF16), "dp", scatter_dimension=0, tiled=True
    )
    own_state = small_sum[:, : state // 2]
    other_state = swap(own_state)
    state_sum = jnp.where(
        first_core,
        jnp.concatenate([own_state, other_state], axis=1),
        jnp.concatenate([other_state, own_state], axis=1),
    )

    def head_row(number):
        inner_grad = back["inner_grad"][number]
        skip = jnp.sum(inner_grad[6].reshape(heads, head_dim), axis=1)
        lanes = slice(number * heads, (number + 1) * heads)
        return jnp.concatenate(
            [
                inner_grad[:6],
                pad_lanes(
                    jnp.concatenate(
                        [skip, back["head_grad"][0, lanes], back["head_grad"][1, lanes]]
                    )[None],
                    half,
                ),
            ],
            axis=0,
        )

    common = jnp.concatenate(
        [
            back["norm_grad"],
            pad_lanes(
                jnp.concatenate(
                    [back["state_grad"][number : number + 1] for number in range(5)], axis=1
                ).reshape(1, -1),
                2 * width,
            ).reshape(2, width),
        ],
        axis=0,
    )
    small = jnp.concatenate([head_row(0), common], axis=0) + swap(
        jnp.concatenate([head_row(1), common], axis=0)
    )
    small = lax.psum(small, "dp")
    share = width // lax.axis_size("dp")
    norm_gain_grad = lax.dynamic_slice_in_dim(small[7:8], lax.axis_index("dp") * share, share, 1)
    state_small = small[8:10].reshape(-1)[: 5 * state].reshape(5, state)
    return (
        section_output[None],
        input_grad[None],
        norm_gain_grad,
        in_sum.astype(F32).reshape(1, share, 2, half),
        state_sum.astype(F32)[None],
        small_sum[:, state // 2 :].astype(F32)[None],
        small[0:4][None],
        small[4:5],
        state_small[None, :4],
        state_small[4:5],
        small[6:7, heads : 2 * heads],
        small[6:7, 2 * heads : 3 * heads],
        small[6:7, :heads],
        small[5:6],
        out_sum.astype(F32).T[None],
    )


def solution(mesh):
    placed = (
        P(None, "dp", None),
        P(None, "dp", None),
        P("section", None),
        P("section", None, None, "tensor"),
        P("section", None, None),
        P("section", None, "tensor"),
        P("section", None, "tensor"),
        P("section", "tensor"),
        P("section", None, None),
        P("section", None),
        P("section", "tensor"),
        P("section", "tensor"),
        P("section", "tensor"),
        P("section", "tensor"),
        P("section", "tensor", None),
        P(None, "dp", None),
    )
    return jax.shard_map(
        local,
        mesh=mesh,
        in_specs=placed,
        out_specs=(
            P("section", None, "dp", None),
            P("section", None, "dp", None),
            P("section", "dp"),
            P("section", "dp", None, "tensor"),
            P("section", "dp", None),
            P("section", "dp", "tensor"),
            P("section", None, "tensor"),
            P("section", "tensor"),
            P("section", None, None),
            P("section", None),
            P("section", "tensor"),
            P("section", "tensor"),
            P("section", "tensor"),
            P("section", "tensor"),
            P("section", "tensor", "dp"),
        ),
        check_vma=False,
    )
```

```python
from types import SimpleNamespace

import jax
import jax.numpy as jnp
from jax import lax
from jax.experimental import pallas as pl
from jax.experimental.pallas import tpu as pltpu
from jax.sharding import PartitionSpec as P

EPS = 1e-05
LANES = 128
BLOCK = 256
HEAD_DIM = 64
NT = (((1,), (1,)), ((), ()))
TN = (((0,), (0,)), ((), ()))
F32 = jnp.float32
BF16 = jnp.bfloat16


def matmul(left, right):
    return jnp.dot(left, right, preferred_element_type=F32)


def matmul_nt(left, right):
    return lax.dot_general(left, right, NT, preferred_element_type=F32)


def matmul_tn(left, right):
    return lax.dot_general(left, right, TN, preferred_element_type=F32)


def down(values, steps):
    return pltpu.roll(values, steps, 0)


def up(values, steps):
    return pltpu.roll(values, values.shape[0] - steps, 0)


def col_sum(values):
    return jnp.sum(values, axis=0, keepdims=True)


def fold(values):
    total = values[:, :LANES]
    for start in range(LANES, values.shape[1], LANES):
        total = total + values[:, start : start + LANES]
    return total


class Row:
    def __init__(self, lengths_ref, rows):
        wide = (rows, BLOCK)
        place = lax.broadcasted_iota(jnp.int32, wide, 0)
        lane = lax.broadcasted_iota(jnp.int32, (rows, rows), 1)
        segment = jnp.zeros(wide, jnp.int32)
        segment_lane = jnp.zeros((rows, rows), jnp.int32)
        end = jnp.int32(0)
        for number in range(lengths_ref.shape[1]):
            end = end + lengths_ref[0, number]
            segment = segment + jnp.where(place >= end, 1, 0)
            segment_lane = segment_lane + jnp.where(lane >= end, 1, 0)
        self.rows = rows
        self.allowed = (place[:, :rows] >= lane) & (segment[:, :rows] == segment_lane)
        self.place = place[:, :LANES]
        self.same = [None]
        for steps in range(1, 4):
            kept = (place >= steps) & (segment == down(segment, steps))
            self.same.append(jnp.where(kept, 1.0, 0.0).astype(F32))


def conv_pre(row, values, taps, bias):
    kernel = len(taps)
    running = bias + taps[kernel - 1] * values
    for steps in range(1, kernel):
        running = running + taps[kernel - 1 - steps] * (row.same[steps] * down(values, steps))
    return running


def conv_back(row, d_pre, values, taps):
    kernel = len(taps)
    d_values = taps[kernel - 1] * d_pre
    d_taps = [None] * kernel
    d_taps[kernel - 1] = col_sum(d_pre * values)
    for steps in range(1, kernel):
        masked = row.same[steps] * d_pre
        d_values = d_values + taps[kernel - 1 - steps] * up(masked, steps)
        d_taps[kernel - 1 - steps] = col_sum(masked * down(values, steps))
    return d_values, d_taps, col_sum(d_pre)


def silu_back(pre, sig):
    return sig * (1.0 + pre * (1.0 - sig))


def softplus(values):
    return jnp.maximum(values, 0.0) + jnp.log1p(jnp.exp(-jnp.abs(values)))


def running_sum(row, values):
    steps = 1
    while steps < row.rows:
        values = values + jnp.where(row.place >= steps, down(values, steps), 0.0)
        steps *= 2
    return values


def running_sum_back(row, values):
    steps = 1
    while steps < row.rows:
        values = values + jnp.where(row.place < row.rows - steps, up(values, steps), 0.0)
        steps *= 2
    return values


def block_at(index):
    return pl.ds(pl.multiple_of(index * BLOCK, BLOCK), BLOCK)


def split_heads(values, low):
    return jnp.concatenate(
        [jnp.where(low, values, 0.0), jnp.where(low, 0.0, values)], axis=0
    ).astype(BF16)


def tap_rows(ref, where):
    return [ref[number : number + 1, where] for number in range(4)]


def mixer_inputs(row, k):
    state_pre = k.state_pre[...]
    taps = [k.state_par[number : number + 1, :] for number in range(4)]
    pre = conv_pre(row, state_pre, taps, k.state_par[4:5, :])
    sig = jax.nn.sigmoid(pre)
    state_q = (pre * sig).astype(BF16)
    half = state_q.shape[1] // 2
    in_state, out_state = state_q[:, :half], state_q[:, half:]
    step_in = k.step_raw[...] + k.head_par[0:1, :]
    step = softplus(step_in)
    rate = -jnp.exp(k.head_par[1:2, :])
    cumulated = running_sum(row, step * rate)
    return SimpleNamespace(
        pre=pre,
        sig=sig,
        taps=taps,
        state_pre=state_pre,
        in_state=in_state,
        out_state=out_state,
        scores=matmul_nt(out_state, in_state),
        step_in=step_in,
        step=step,
        rate=rate,
        cumulated=cumulated,
    )


def decay_of(row, rolled, k, first, number):
    head = first + number
    spread = rolled[:, number : number + 1] - k.cum_t[pl.ds(head, 1), :]
    decay = jnp.exp(jnp.where(row.allowed, spread, -1e30))
    return head, decay, k.step_t[pl.ds(head, 1), :]


def norm_parts(k):
    residual = k.x[...].astype(F32)
    width = residual.shape[1]
    inverse = lax.rsqrt(jnp.sum(residual * residual, axis=1, keepdims=True) / width + EPS)
    return residual, inverse, (residual * inverse * k.norm_par[...]).astype(BF16)


def sizes(k):
    inner = k.inner_par.shape[1]
    per_block = BLOCK // HEAD_DIM
    return inner, inner // 2, per_block, inner // 2 // BLOCK


def forward(row, k, load):
    rows = row.rows
    inner, local, per_block, half_blocks = sizes(k)
    _, _, normed = norm_parts(k)
    k.normed[...] = normed
    load.state.wait()
    k.state_pre[...] = matmul(normed, k.w_state[...])
    k.step_raw[...] = matmul(normed, k.w_step[...])
    mixer = mixer_inputs(row, k)
    k.step_t[...] = mixer.step.T
    k.cum_t[...] = mixer.cumulated.T
    scores, cumulated = mixer.scores, mixer.cumulated
    low = lax.broadcasted_iota(jnp.int32, (rows, LANES), 1) < HEAD_DIM

    def body(index, squares):
        where = block_at(index)
        half = index // half_blocks
        start = half * (2 * half_blocks) + (index - half * half_blocks)
        gate = matmul(k.normed[...], k.w_in[:, block_at(start)])
        value = matmul(k.normed[...], k.w_in[:, block_at(start + half_blocks)])
        k.gate[:, where] = gate
        k.inner[:, where] = value
        pre = conv_pre(row, value, tap_rows(k.inner_par, where), k.inner_par[4:5, where])
        act = pre * jax.nn.sigmoid(pre)
        first = index * per_block
        rolled = pltpu.roll(cumulated, LANES - first, 1)
        outs = []
        for pair in range(per_block // 2):
            mixes = []
            for number in (2 * pair, 2 * pair + 1):
                _, decay, step_row = decay_of(row, rolled, k, first, number)
                mixes.append((scores * decay * step_row).astype(BF16))
            values = split_heads(act[:, pair * LANES : (pair + 1) * LANES], low)
            outs.append(matmul(jnp.concatenate(mixes, axis=1), values))
        ssd = jnp.concatenate(outs, axis=1) + k.inner_par[6:7, where] * act
        k.ssd[:, where] = ssd
        raw = ssd * gate * jax.nn.sigmoid(gate)
        return squares + fold(raw * raw)

    load.own.wait()
    squares = lax.fori_loop(0, half_blocks, body, jnp.zeros((rows, LANES), F32))
    load.other.wait()
    squares = lax.fori_loop(half_blocks, 2 * half_blocks, body, squares)
    inverse = lax.rsqrt(jnp.sum(squares, axis=1, keepdims=True) / inner + EPS)
    k.inverse[...] = jnp.broadcast_to(inverse, (rows, LANES))

    for half, target in enumerate((k.gated_own, k.gated_other)):

        def normalize(index, carry):
            where = block_at(index + half * half_blocks)
            gate = k.gate[:, where]
            raw = k.ssd[:, where] * gate * jax.nn.sigmoid(gate)
            target[:, block_at(index)] = (raw * inverse * k.inner_par[5:6, where]).astype(BF16)
            return carry

        lax.fori_loop(0, half_blocks, normalize, 0)
    load.out.wait()

    def project(index, carry):
        where = block_at(index)
        total = matmul(k.gated_own[...], k.w_out[:local, where])
        total = total + matmul(k.gated_other[...], k.w_out[local:, where])
        k.result[:, where] = (k.x[:, where].astype(F32) + total).astype(BF16)
        return carry

    lax.fori_loop(0, k.result.shape[1] // BLOCK, project, 0)


def store_half(index, half_blocks, own, other, value):
    @pl.when(index < half_blocks)
    def _():
        own[:, block_at(index)] = value

    @pl.when(index >= half_blocks)
    def _():
        other[:, block_at(index - half_blocks)] = value


def gate_back(row, k, load, full):
    inner, local, per_block, half_blocks = sizes(k)
    inverse = k.inverse[:, 0:1]
    load.out.wait()

    def spread_grad(index, total):
        where = block_at(index)
        gate = k.gate[:, where]
        raw = k.ssd[:, where] * gate * jax.nn.sigmoid(gate)
        d_gated_n = matmul_nt(k.grad_in[...], k.w_out[where, :])
        k.d_ssd[:, where] = d_gated_n
        if full:
            gain = col_sum(d_gated_n * raw * inverse)
            store_half(index, half_blocks, k.gain_own, k.gain_other, gain)
        return total + fold(d_gated_n * k.inner_par[5:6, where] * raw)

    zero = jnp.zeros((row.rows, LANES), F32)
    total = lax.fori_loop(0, 2 * half_blocks, spread_grad, zero)
    pull = inverse * inverse * inverse * jnp.sum(total, axis=1, keepdims=True) / inner

    def body(index, carry):
        where = block_at(index)
        gate = k.gate[:, where]
        ssd = k.ssd[:, where]
        sig = jax.nn.sigmoid(gate)
        act_gate = gate * sig
        d_gated = inverse * k.inner_par[5:6, where] * k.d_ssd[:, where] - ssd * act_gate * pull
        k.d_ssd[:, where] = d_gated * act_gate
        d_gate = (d_gated * ssd * silu_back(gate, sig)).astype(BF16)
        store_half(index, half_blocks, k.d_gate_own, k.d_gate_other, d_gate)
        return carry

    lax.fori_loop(0, 2 * half_blocks, body, 0)


def mix_back(row, k, full):
    rows = row.rows
    inner, local, per_block, half_blocks = sizes(k)
    mixer = mixer_inputs(row, k)
    k.step_t[...] = mixer.step.T
    k.cum_t[...] = mixer.cumulated.T
    scores, cumulated = mixer.scores, mixer.cumulated
    lane = lax.broadcasted_iota(jnp.int32, (rows, LANES), 1)
    low = lane < HEAD_DIM

    def body(index, carry):
        d_scores, row_sums = carry
        where = block_at(index)
        d_ssd = k.d_ssd[:, where]
        value = k.inner[:, where]
        taps = tap_rows(k.inner_par, where)
        pre = conv_pre(row, value, taps, k.inner_par[4:5, where])
        pre_sig = jax.nn.sigmoid(pre)
        act = pre * pre_sig
        first = index * per_block
        rolled = pltpu.roll(cumulated, LANES - first, 1)
        d_inner = []
        for pair in range(per_block // 2):
            lanes = slice(pair * LANES, (pair + 1) * LANES)
            values = split_heads(act[:, lanes], low)
            d_pair = d_ssd[:, lanes]
            d_mix = matmul_nt(d_pair.astype(BF16), values)
            mixes = []
            for place in range(2):
                head, decay, step_row = decay_of(row, rolled, k, first, 2 * pair + place)
                part = d_mix[:, place * rows : (place + 1) * rows] * decay
                weighted = part * step_row
                d_scores = d_scores + weighted
                k.d_col[pl.ds(head, 1), :] = col_sum(part * scores)
                row_sum = jnp.sum(weighted * scores, axis=1, keepdims=True)
                row_sums = jnp.where(lane == head, row_sum, row_sums)
                mixes.append((scores * decay * step_row).astype(BF16))
            d_inner.append(matmul_tn(jnp.concatenate(mixes, axis=0), split_heads(d_pair, low)))
        d_act = jnp.concatenate(d_inner, axis=1) + k.inner_par[6:7, where] * d_ssd
        d_value, d_taps, d_bias = conv_back(row, d_act * silu_back(pre, pre_sig), value, taps)
        store_half(index, half_blocks, k.d_value_own, k.d_value_other, d_value.astype(BF16))
        if full:
            grads = jnp.concatenate(
                [*d_taps, d_bias, jnp.zeros_like(d_bias), col_sum(d_ssd * act), jnp.zeros_like(d_bias)],
                axis=0,
            )
            store_half(index, half_blocks, k.conv_own, k.conv_other, grads)
        return d_scores, row_sums

    zero = jnp.zeros((rows, LANES), F32)
    k.d_col[...] = jnp.zeros(k.d_col.shape, F32)
    d_scores, row_sums = lax.fori_loop(0, 2 * half_blocks, body, (zero, zero))
    k.d_scores[...] = d_scores
    k.row_sums[...] = row_sums


def input_back(row, k, load, full):
    inner, local, per_block, half_blocks = sizes(k)
    heads = local // HEAD_DIM
    mixer = mixer_inputs(row, k)
    d_col = k.d_col[...]
    d_cumulated = k.row_sums[...] - (d_col * mixer.step.T).T
    d_scaled = running_sum_back(row, d_cumulated)
    d_step = d_col.T + d_scaled * mixer.rate
    d_step_raw = d_step * jax.nn.sigmoid(mixer.step_in)
    d_step_q = d_step_raw.astype(BF16)
    d_scores_q = k.d_scores[...].astype(BF16)
    d_state_act = jnp.concatenate(
        [matmul_tn(d_scores_q, mixer.out_state), matmul(d_scores_q, mixer.in_state)], axis=1
    )
    d_state, d_taps, d_bias = conv_back(
        row, d_state_act * silu_back(mixer.pre, mixer.sig), mixer.state_pre, mixer.taps
    )
    d_state_q = d_state.astype(BF16)
    load.state.wait()
    load.own.wait()
    load.other.wait()
    residual, inverse_norm, _ = norm_parts(k)
    k.d_normed[...] = matmul_nt(d_step_q, k.w_step[...]) + matmul_nt(d_state_q, k.w_state[...])
    width = residual.shape[1]

    def project(index, carry):
        where = block_at(index)
        total = k.d_normed[:, where]
        parts = (k.d_gate_own, k.d_value_own, k.d_gate_other, k.d_value_other)
        for number, part in enumerate(parts):
            span = slice(number * local, (number + 1) * local)
            total = total + matmul_nt(part[...], k.w_in[where, span])
        k.d_normed[:, where] = total
        return carry

    lax.fori_loop(0, width // BLOCK, project, 0)
    d_normed = k.d_normed[...]
    scaled = d_normed * k.norm_par[...]
    mean = jnp.sum(scaled * residual, axis=1, keepdims=True) / width
    d_residual = inverse_norm * scaled - residual * (
        inverse_norm * inverse_norm * inverse_norm * mean
    )
    input_grad = k.grad_in[...].astype(F32) + d_residual
    k.grad[...] = input_grad.astype(k.grad.dtype)
    if not full:
        return
    half = d_state_q.shape[1] // 2
    is_first = k.core[0, 0] == 0
    low_half, high_half = d_state[:, :half], d_state[:, half:]
    pairs = (
        (k.small_own, jnp.where(is_first, low_half, high_half), d_step_raw),
        (
            k.small_other,
            jnp.where(is_first, high_half, low_half),
            pltpu.roll(d_step_raw, LANES - heads, 1),
        ),
    )
    for target, state_part, step_part in pairs:
        target[...] = jnp.concatenate([state_part, step_part], axis=1).astype(BF16)
    bias_grad = col_sum(d_step_raw)
    decay_grad = col_sum(d_scaled * mixer.step) * mixer.rate
    lane = lax.broadcasted_iota(jnp.int32, bias_grad.shape, 1)
    norm_grad = col_sum(d_normed * residual * inverse_norm)
    state_row = jnp.concatenate(d_taps, axis=1)
    for number, (target, gain, conv) in enumerate(
        ((k.pack_own, k.gain_own, k.conv_own), (k.pack_other, k.gain_other, k.conv_other))
    ):
        target[...] = jnp.zeros(target.shape, F32)
        target[0:5, :] = conv[0:5, :]
        target[5:6, :] = gain[...]
        target[6:7, :] = conv[6:7, :]
        bias_part, decay_part = bias_grad, pltpu.roll(decay_grad, heads, 1)
        if number == 1:
            bias_part, decay_part = pltpu.roll(bias_grad, LANES - heads, 1), decay_grad
        head_row = jnp.where(lane < heads, bias_part, decay_part)
        target[7:8, 0:LANES] = head_row
        target[8:9, :] = norm_grad
        target[9:10, 0 : state_row.shape[1]] = state_row
        target[10:11, 0 : d_bias.shape[1]] = d_bias


class Load:
    def __init__(self):
        self.copies = []
        self.waited = False

    def start(self, source, target, sem):
        copy = pltpu.make_async_copy(source, target, sem)
        copy.start()
        self.copies.append(copy)

    def wait(self):
        if not self.waited:
            self.waited = True
            for copy in self.copies:
                copy.wait()


def start_loads(k, inward, outward, out_first):
    load = SimpleNamespace(state=Load(), own=Load(), other=Load(), out=Load())

    def start_out():
        rows = k.own_out.shape[0]
        load.out.start(k.own_out, k.w_out.at[pl.ds(0, rows), :], k.sems.at[0])
        load.out.start(k.other_out, k.w_out.at[pl.ds(rows, rows), :], k.sems.at[1])

    if outward and out_first:
        start_out()
    if inward:
        columns = k.own_in.shape[1]
        load.state.start(k.state_w, k.w_state, k.sems.at[2])
        load.state.start(k.step_w, k.w_step, k.sems.at[3])
        load.own.start(k.own_in, k.w_in.at[:, pl.ds(0, columns)], k.sems.at[4])
        load.other.start(k.other_in, k.w_in.at[:, pl.ds(columns, columns)], k.sems.at[5])
    if outward and not out_first:
        start_out()
    return load


def run_kernel(body, inputs, outputs, scratch, flops, moved):
    names = [*inputs, *outputs, *scratch]
    vmem = pl.BlockSpec(memory_space=pltpu.VMEM)
    smem = pl.BlockSpec(memory_space=pltpu.SMEM)
    anywhere = pl.BlockSpec(memory_space=pl.ANY)

    def spec(value):
        if value.dtype == jnp.int32:
            return smem
        return anywhere if value.size * value.dtype.itemsize >= 1 << 22 or value.shape[0] >= 1024 else vmem

    def kernel(*refs):
        body(SimpleNamespace(**dict(zip(names, refs[: len(names)])), sems=refs[-1]))

    results = pl.pallas_call(
        kernel,
        name=body.__name__,
        out_shape=[jax.ShapeDtypeStruct(*shape) for shape in outputs.values()],
        in_specs=[spec(value) for value in inputs.values()],
        out_specs=[vmem for _ in outputs],
        scratch_shapes=[pltpu.VMEM(*shape) for shape in scratch.values()]
        + [pltpu.SemaphoreType.DMA((6,))],
        compiler_params=pltpu.CompilerParams(vmem_limit_bytes=48 << 20),
        cost_estimate=pl.CostEstimate(flops=flops, bytes_accessed=moved, transcendentals=0),
    )(*inputs.values())
    return dict(zip(outputs, results))


def swap_core(value):
    return lax.ppermute(value, "tensor", [(0, 1), (1, 0)])


def swap_bit(value, bit):
    count = lax.axis_size("dp")
    return lax.ppermute(value, "dp", [(place, place ^ bit) for place in range(count)])


def swap_both(value):
    count, cores = lax.axis_size("dp"), lax.axis_size("tensor")
    pairs = [
        (place * cores + core, (place ^ 1) * cores + (core ^ 1))
        for place in range(count)
        for core in range(cores)
    ]
    return lax.ppermute(value, ("dp", "tensor"), pairs)


def to_section(value, source, target):
    return lax.ppermute(value, "section", [(source, target)])


def in_order(own, other, first):
    return jnp.where(first, jnp.stack([own, other]), jnp.stack([other, own]))


def four_rows(own, core_part, x_part, both_part):
    return jnp.concatenate(
        [own, swap_core(core_part), swap_bit(x_part, 1), swap_both(both_part)], axis=0
    )


def halves_of_four(own, other):
    return four_rows(own, other, own, other)


def arranged(values):
    place = lax.axis_index("dp")
    count = lax.axis_size("dp")
    bits = count.bit_length() - 1
    rows, width = values.shape
    shape = (rows,) + (2,) * bits + (width // count,)
    values = values.reshape(shape)
    for bit in range(bits):
        axis = bits - bit
        values = jnp.where((place >> bit) & 1 == 1, jnp.flip(values, axis), values)
    order = (bits,) + (0,) + tuple(range(bits - 1, 0, -1)) + (bits + 1,)
    values = jnp.transpose(values, order).reshape(2, rows, width // 2)
    return values[0], values[1]


def dp_sums(left, right):
    count = lax.axis_size("dp")
    rows = left.shape[1]
    bit = 2
    total = None
    while bit < count:
        rows //= 2
        if total is None:
            sent = matmul_tn(left[:, rows:], right).astype(BF16)
            kept = matmul_tn(left[:, :rows], right)
        else:
            sent, kept = total[rows:].astype(BF16), total[:rows]
        total = kept + swap_bit(sent, bit).astype(F32)
        bit *= 2
    return total


def dp_total(value):
    bit = 1
    while bit < lax.axis_size("dp"):
        value = value + swap_bit(value, bit)
        bit *= 2
    return value


def local(
    block_input,
    seq_lengths,
    norm_gain,
    in_weight,
    state_weight,
    step_weight,
    conv_weight,
    conv_bias,
    state_conv,
    state_bias,
    step_bias,
    decay_log,
    skip_gain,
    gate_gain,
    out_weight,
    out_cotangent,
):
    core = lax.axis_index("tensor")
    first_core = core == 0
    first_section = lax.axis_index("section") == 0
    rows = block_input.shape[1]
    width, _, half = in_weight.shape[1:]
    inner = 2 * half
    heads = step_weight.shape[2]
    state = state_weight.shape[2]
    own_in = in_weight[0].reshape(width, inner)
    other_in = swap_core(own_in)
    own_out = out_weight[0]
    other_out = swap_core(own_out)
    own_step = step_weight[0]
    other_step = swap_core(own_step)
    own_par = jnp.concatenate(
        [
            conv_weight[0],
            conv_bias,
            gate_gain,
            jnp.repeat(skip_gain, HEAD_DIM, axis=1),
            jnp.concatenate(
                [step_bias, decay_log, jnp.zeros((1, half - 2 * heads), F32)], axis=1
            ),
        ],
        axis=0,
    )
    other_par = swap_core(own_par)

    def pad_lanes(value, lanes):
        return jnp.pad(value, ((0, 0), (0, lanes - value.shape[1])))

    def head_row(start):
        lanes = slice(start, start + heads)
        return pad_lanes(jnp.concatenate([own_par[7:8, lanes], other_par[7:8, lanes]], 1), LANES)

    lengths = dict(lengths=lax.dynamic_slice_in_dim(seq_lengths[:, 0], core, 1, axis=0))
    norm_par = dict(norm_par=norm_gain)
    inner_par = dict(inner_par=jnp.concatenate([own_par, other_par], axis=1))
    mixer_par = dict(
        state_par=jnp.concatenate([state_conv[0], state_bias, jnp.zeros((3, state), F32)], axis=0),
        head_par=jnp.concatenate([head_row(0), head_row(heads), jnp.zeros((6, LANES), F32)], axis=0),
    )
    inward = dict(
        own_in=own_in,
        other_in=other_in,
        state_w=state_weight[0],
        step_w=pad_lanes(jnp.concatenate([own_step, other_step], axis=1), LANES),
    )
    outward = dict(own_out=own_out, other_out=other_out)
    inward_scratch = dict(
        w_in=((width, 2 * inner), BF16),
        w_state=((width, state), BF16),
        w_step=((width, LANES), BF16),
    )
    outward_scratch = dict(w_out=((inner, width), BF16))
    turned = dict(step_t=((LANES, rows), F32), cum_t=((LANES, rows), F32))
    kept_shapes = dict(
        normed=((rows, width), BF16),
        gate=((rows, inner), F32),
        inner=((rows, inner), F32),
        ssd=((rows, inner), F32),
        state_pre=((rows, state), F32),
        step_raw=((rows, LANES), F32),
        inverse=((rows, LANES), F32),
        gated_own=((rows, half), BF16),
        gated_other=((rows, half), BF16),
    )
    gate_shapes = dict(
        d_ssd=((rows, inner), F32),
        d_gate_own=((rows, half), BF16),
        d_gate_other=((rows, half), BF16),
    )
    mix_shapes = dict(
        d_value_own=((rows, half), BF16),
        d_value_other=((rows, half), BF16),
        d_col=((LANES, rows), F32),
        d_scores=((rows, rows), F32),
        row_sums=((rows, LANES), F32),
    )
    gains = dict(gain_own=((1, half), F32), gain_other=((1, half), F32))
    convs = dict(conv_own=((8, half), F32), conv_other=((8, half), F32))
    normed_grad = dict(d_normed=((rows, width), F32))
    result = dict(result=((rows, width), BF16))
    work = 2 * rows * width * inner
    weight_bytes = 2 * width * inner

    def forward_pass(k):
        forward(Row(k.lengths, rows), k, start_loads(k, True, True, False))

    def both_passes(k):
        load = start_loads(k, True, True, False)
        row = Row(k.lengths, rows)
        forward(row, k, load)
        gate_back(row, k, load, False)
        mix_back(row, k, False)
        input_back(row, k, load, False)

    def gate_pass(k):
        gate_back(SimpleNamespace(rows=rows), k, start_loads(k, False, True, True), True)

    def mix_pass(k):
        mix_back(Row(k.lengths, rows), k, True)

    def input_pass(k):
        input_back(Row(k.lengths, rows), k, start_loads(k, True, False, False), True)

    first_input = lax.dynamic_index_in_dim(block_input, core, 0, keepdims=False)
    cotangent = lax.dynamic_index_in_dim(out_cotangent, core, 0, keepdims=False)
    shared = {**lengths, **norm_par, **inner_par, **mixer_par, **inward, **outward}
    weights = {**inward_scratch, **outward_scratch}

    middle = run_kernel(
        forward_pass,
        dict(x=first_input, **shared),
        result,
        {**kept_shapes, **turned, **weights},
        3 * work,
        3 * weight_bytes,
    )
    carried = to_section(middle["result"], 0, 1)
    hidden = dict(x=jnp.where(first_section, first_input, carried))
    kept = run_kernel(
        both_passes,
        {**hidden, **shared, **dict(grad_in=cotangent)},
        {**result, **kept_shapes, **dict(grad=((rows, width), BF16))},
        {**turned, **gate_shapes, **mix_shapes, **normed_grad, **weights},
        6 * work,
        3 * weight_bytes,
    )
    keep = SimpleNamespace(**kept)
    normed_here, normed_there = arranged(keep.normed)
    normed = four_rows(normed_here, normed_here, normed_there, normed_there)
    gated_n = halves_of_four(keep.gated_own, keep.gated_other)
    section_output = in_order(keep.result, swap_core(keep.result), first_core)

    grad_carried = to_section(keep.grad, 1, 0)
    grad_in = dict(grad_in=jnp.where(first_section, grad_carried, cotangent))
    gated = run_kernel(
        gate_pass,
        {
            **grad_in,
            **inner_par,
            **outward,
            **dict(gate=keep.gate, ssd=keep.ssd, inverse=keep.inverse),
        },
        {**gate_shapes, **gains},
        outward_scratch,
        work,
        weight_bytes,
    )
    gated_ns = SimpleNamespace(**gated)
    grad_here, grad_there = arranged(grad_in["grad_in"])
    grad_q = four_rows(grad_here, grad_here, grad_there, grad_there)
    d_gate = halves_of_four(gated_ns.d_gate_own, gated_ns.d_gate_other)
    out_sum = dp_sums(grad_q, gated_n)
    mixer_kept = dict(state_pre=keep.state_pre, step_raw=keep.step_raw)
    mixed = run_kernel(
        mix_pass,
        {
            **lengths,
            **inner_par,
            **mixer_par,
            **mixer_kept,
            **dict(inner=keep.inner, d_ssd=gated_ns.d_ssd),
        },
        {**mix_shapes, **convs},
        turned,
        work,
        weight_bytes,
    )
    mixed_ns = SimpleNamespace(**mixed)
    d_value = halves_of_four(mixed_ns.d_value_own, mixed_ns.d_value_other)
    gate_sum = dp_sums(normed, d_gate)
    back = SimpleNamespace(
        **run_kernel(
            input_pass,
            {
                **hidden,
                **lengths,
                **dict(core=core.astype(jnp.int32).reshape(1, 1)),
                **norm_par,
                **inner_par,
                **mixer_par,
                **mixer_kept,
                **inward,
                **grad_in,
                **dict(d_gate_own=gated_ns.d_gate_own, d_gate_other=gated_ns.d_gate_other),
                **dict(gain_own=gated_ns.gain_own, gain_other=gated_ns.gain_other),
                **mixed,
            },
            dict(
                grad=((rows, width), F32),
                small_own=((rows, 2 * LANES), BF16),
                small_other=((rows, 2 * LANES), BF16),
                pack_own=((16, half), F32),
                pack_other=((16, half), F32),
            ),
            {**normed_grad, **inward_scratch},
            2 * work,
            2 * weight_bytes,
        )
    )
    value_sum = dp_sums(normed, d_value)
    small_sum = dp_sums(normed, halves_of_four(back.small_own, back.small_other))
    input_grad = in_order(back.grad, swap_core(back.grad), first_core)
    small = dp_total(back.pack_own + swap_core(back.pack_other))

    own_state = small_sum[:, : state // 2]
    other_state = swap_core(own_state)
    state_sum = jnp.where(
        first_core,
        jnp.concatenate([own_state, other_state], axis=1),
        jnp.concatenate([other_state, own_state], axis=1),
    )
    share = width // lax.axis_size("dp")
    return (
        section_output[None],
        input_grad[None],
        lax.dynamic_slice_in_dim(small[8:9], lax.axis_index("dp") * share, share, 1),
        jnp.stack([gate_sum, value_sum], axis=1)[None],
        state_sum[None],
        small_sum[:, state // 2 : state // 2 + heads][None],
        small[0:4][None],
        small[4:5],
        small[9, : 4 * state].reshape(1, 4, state),
        small[10:11, :state],
        small[7:8, :heads],
        small[7:8, heads : 2 * heads],
        jnp.sum(small[6].reshape(1, heads, HEAD_DIM), axis=2),
        small[5:6],
        out_sum.T[None],
    )


def solution(mesh):
    per_row = P(None, "dp", None)
    by_section = P("section", None)
    by_core = P("section", "tensor")
    columns = P("section", None, "tensor")
    whole = P("section", None, None)
    rows_out = P("section", None, "dp", None)
    return jax.shard_map(
        local,
        mesh=mesh,
        in_specs=(
            per_row,
            per_row,
            by_section,
            P("section", None, None, "tensor"),
            whole,
            columns,
            columns,
            by_core,
            whole,
            by_section,
            by_core,
            by_core,
            by_core,
            by_core,
            P("section", "tensor", None),
            per_row,
        ),
        out_specs=(
            rows_out,
            rows_out,
            P("section", "dp"),
            P("section", "dp", None, "tensor"),
            P("section", "dp", None),
            P("section", "dp", "tensor"),
            columns,
            by_core,
            whole,
            by_section,
            by_core,
            by_core,
            by_core,
            by_core,
            P("section", "tensor", "dp"),
        ),
        check_vma=False,
    )
```

```python
from types import SimpleNamespace

import jax
import jax.numpy as jnp
from jax import lax
from jax.experimental import pallas as pl
from jax.experimental.pallas import tpu as pltpu
from jax.sharding import PartitionSpec as P

EPS = 1e-05
LANES = 128
BLOCK = 256
HEAD_DIM = 64
NT = (((1,), (1,)), ((), ()))
TN = (((0,), (0,)), ((), ()))
F32 = jnp.float32
BF16 = jnp.bfloat16


def matmul(left, right):
    return jnp.dot(left, right, preferred_element_type=F32)


def matmul_nt(left, right):
    return lax.dot_general(left, right, NT, preferred_element_type=F32)


def matmul_tn(left, right):
    return lax.dot_general(left, right, TN, preferred_element_type=F32)


def down(values, steps):
    return pltpu.roll(values, steps, 0)


def up(values, steps):
    return pltpu.roll(values, values.shape[0] - steps, 0)


def col_sum(values):
    return jnp.sum(values, axis=0, keepdims=True)


def fold(values):
    total = values[:, :LANES]
    for start in range(LANES, values.shape[1], LANES):
        total = total + values[:, start : start + LANES]
    return total


class Row:
    def __init__(self, lengths_ref, rows):
        wide = (rows, BLOCK)
        place = lax.broadcasted_iota(jnp.int32, wide, 0)
        lane = lax.broadcasted_iota(jnp.int32, (rows, rows), 1)
        segment = jnp.zeros(wide, jnp.int32)
        segment_lane = jnp.zeros((rows, rows), jnp.int32)
        end = jnp.int32(0)
        for number in range(lengths_ref.shape[1]):
            end = end + lengths_ref[0, number]
            segment = segment + jnp.where(place >= end, 1, 0)
            segment_lane = segment_lane + jnp.where(lane >= end, 1, 0)
        self.rows = rows
        self.allowed = (place[:, :rows] >= lane) & (segment[:, :rows] == segment_lane)
        self.place = place[:, :LANES]
        self.same = [None]
        for steps in range(1, 4):
            kept = (place >= steps) & (segment == down(segment, steps))
            self.same.append(jnp.where(kept, 1.0, 0.0).astype(F32))


def conv_pre(row, values, taps, bias):
    kernel = len(taps)
    running = bias + taps[kernel - 1] * values
    for steps in range(1, kernel):
        running = running + taps[kernel - 1 - steps] * (row.same[steps] * down(values, steps))
    return running


def conv_back(row, d_pre, values, taps):
    kernel = len(taps)
    d_values = taps[kernel - 1] * d_pre
    d_taps = [None] * kernel
    d_taps[kernel - 1] = col_sum(d_pre * values)
    for steps in range(1, kernel):
        masked = row.same[steps] * d_pre
        d_values = d_values + taps[kernel - 1 - steps] * up(masked, steps)
        d_taps[kernel - 1 - steps] = col_sum(masked * down(values, steps))
    return d_values, d_taps, col_sum(d_pre)


def silu_back(pre, sig):
    return sig * (1.0 + pre * (1.0 - sig))


def softplus(values):
    return jnp.maximum(values, 0.0) + jnp.log1p(jnp.exp(-jnp.abs(values)))


def running_sum(row, values):
    steps = 1
    while steps < row.rows:
        values = values + jnp.where(row.place >= steps, down(values, steps), 0.0)
        steps *= 2
    return values


def running_sum_back(row, values):
    steps = 1
    while steps < row.rows:
        values = values + jnp.where(row.place < row.rows - steps, up(values, steps), 0.0)
        steps *= 2
    return values


def block_at(index):
    return pl.ds(pl.multiple_of(index * BLOCK, BLOCK), BLOCK)


def split_heads(values, low):
    return jnp.concatenate(
        [jnp.where(low, values, 0.0), jnp.where(low, 0.0, values)], axis=0
    ).astype(BF16)


def tap_rows(ref, where):
    return [ref[number : number + 1, where] for number in range(4)]


def mixer_inputs(row, k):
    state_pre = k.state_pre[...]
    taps = [k.state_par[number : number + 1, :] for number in range(4)]
    pre = conv_pre(row, state_pre, taps, k.state_par[4:5, :])
    sig = jax.nn.sigmoid(pre)
    state_q = (pre * sig).astype(BF16)
    half = state_q.shape[1] // 2
    in_state, out_state = state_q[:, :half], state_q[:, half:]
    step_in = k.step_raw[...] + k.head_par[0:1, :]
    step = softplus(step_in)
    rate = -jnp.exp(k.head_par[1:2, :])
    cumulated = running_sum(row, step * rate)
    return SimpleNamespace(
        pre=pre,
        sig=sig,
        taps=taps,
        state_pre=state_pre,
        in_state=in_state,
        out_state=out_state,
        scores=matmul_nt(out_state, in_state),
        step_in=step_in,
        step=step,
        rate=rate,
        cumulated=cumulated,
    )


def decay_of(row, rolled, k, first, number):
    head = first + number
    spread = rolled[:, number : number + 1] - k.cum_t[pl.ds(head, 1), :]
    decay = jnp.exp(jnp.where(row.allowed, spread, -1e30))
    return head, decay, k.step_t[pl.ds(head, 1), :]


def norm_parts(k):
    residual = k.x[...].astype(F32)
    width = residual.shape[1]
    inverse = lax.rsqrt(jnp.sum(residual * residual, axis=1, keepdims=True) / width + EPS)
    return residual, inverse, (residual * inverse * k.norm_par[...]).astype(BF16)


def sizes(k):
    inner = k.inner_par.shape[1]
    per_block = BLOCK // HEAD_DIM
    return inner, inner // 2, per_block, inner // 2 // BLOCK


def forward(row, k, load):
    rows = row.rows
    inner, local, per_block, half_blocks = sizes(k)
    _, _, normed = norm_parts(k)
    k.normed[...] = normed
    load.state.wait()
    k.state_pre[...] = matmul(normed, k.w_state[...])
    k.step_raw[...] = matmul(normed, k.w_step[...])
    mixer = mixer_inputs(row, k)
    k.step_t[...] = mixer.step.T
    k.cum_t[...] = mixer.cumulated.T
    scores, cumulated = mixer.scores, mixer.cumulated
    low = lax.broadcasted_iota(jnp.int32, (rows, LANES), 1) < HEAD_DIM

    def body(index, squares):
        where = block_at(index)
        half = index // half_blocks
        start = half * (2 * half_blocks) + (index - half * half_blocks)
        gate = matmul(k.normed[...], k.w_in[:, block_at(start)])
        value = matmul(k.normed[...], k.w_in[:, block_at(start + half_blocks)])
        k.gate[:, where] = gate
        k.inner[:, where] = value
        pre = conv_pre(row, value, tap_rows(k.inner_par, where), k.inner_par[4:5, where])
        act = pre * jax.nn.sigmoid(pre)
        first = index * per_block
        rolled = pltpu.roll(cumulated, LANES - first, 1)
        outs = []
        for pair in range(per_block // 2):
            mixes = []
            for number in (2 * pair, 2 * pair + 1):
                _, decay, step_row = decay_of(row, rolled, k, first, number)
                mixes.append((scores * decay * step_row).astype(BF16))
            values = split_heads(act[:, pair * LANES : (pair + 1) * LANES], low)
            outs.append(matmul(jnp.concatenate(mixes, axis=1), values))
        ssd = jnp.concatenate(outs, axis=1) + k.inner_par[6:7, where] * act
        k.ssd[:, where] = ssd
        raw = ssd * gate * jax.nn.sigmoid(gate)
        return squares + fold(raw * raw)

    load.own.wait()
    squares = lax.fori_loop(0, half_blocks, body, jnp.zeros((rows, LANES), F32))
    load.other.wait()
    squares = lax.fori_loop(half_blocks, 2 * half_blocks, body, squares)
    inverse = lax.rsqrt(jnp.sum(squares, axis=1, keepdims=True) / inner + EPS)
    k.inverse[...] = jnp.broadcast_to(inverse, (rows, LANES))

    aside = k.own_pack.shape[1] - local

    for half, target in enumerate((k.own_pack, k.core_pack)):

        def normalize(index, carry):
            where = block_at(index + half * half_blocks)
            gate = k.gate[:, where]
            raw = k.ssd[:, where] * gate * jax.nn.sigmoid(gate)
            target[:, block_at(index + aside // BLOCK)] = (
                raw * inverse * k.inner_par[5:6, where]
            ).astype(BF16)
            return carry

        lax.fori_loop(0, half_blocks, normalize, 0)
    load.out.wait()

    def project(index, carry):
        where = block_at(index)
        total = matmul(k.own_pack[:, aside:], k.w_out[:local, where])
        total = total + matmul(k.core_pack[:, aside:], k.w_out[local:, where])
        k.result[:, where] = (k.x[:, where].astype(F32) + total).astype(BF16)
        return carry

    lax.fori_loop(0, k.result.shape[1] // BLOCK, project, 0)


def store_half(index, half_blocks, own, other, value, aside=0):
    @pl.when(index < half_blocks)
    def _():
        own[:, block_at(index + aside)] = value

    @pl.when(index >= half_blocks)
    def _():
        other[:, block_at(index - half_blocks + aside)] = value


def gate_back(row, k, load, full):
    inner, local, per_block, half_blocks = sizes(k)
    inverse = k.inverse[:, 0:1]
    aside = (k.own_gate.shape[1] - local) // BLOCK
    load.out.wait()

    def spread_grad(index, total):
        where = block_at(index)
        gate = k.gate[:, where]
        raw = k.ssd[:, where] * gate * jax.nn.sigmoid(gate)
        d_gated_n = matmul_nt(k.grad_in[...], k.w_out[where, :])
        k.d_ssd[:, where] = d_gated_n
        if full:
            gain = col_sum(d_gated_n * raw * inverse)
            store_half(index, half_blocks, k.gain_own, k.gain_other, gain)
        return total + fold(d_gated_n * k.inner_par[5:6, where] * raw)

    zero = jnp.zeros((row.rows, LANES), F32)
    total = lax.fori_loop(0, 2 * half_blocks, spread_grad, zero)
    pull = inverse * inverse * inverse * jnp.sum(total, axis=1, keepdims=True) / inner

    def body(index, carry):
        where = block_at(index)
        gate = k.gate[:, where]
        ssd = k.ssd[:, where]
        sig = jax.nn.sigmoid(gate)
        act_gate = gate * sig
        d_gated = inverse * k.inner_par[5:6, where] * k.d_ssd[:, where] - ssd * act_gate * pull
        k.d_ssd[:, where] = d_gated * act_gate
        d_gate = (d_gated * ssd * silu_back(gate, sig)).astype(BF16)
        store_half(index, half_blocks, k.own_gate, k.core_gate, d_gate, aside)
        return carry

    lax.fori_loop(0, 2 * half_blocks, body, 0)


def mix_back(row, k, full):
    rows = row.rows
    inner, local, per_block, half_blocks = sizes(k)
    mixer = mixer_inputs(row, k)
    k.step_t[...] = mixer.step.T
    k.cum_t[...] = mixer.cumulated.T
    scores, cumulated = mixer.scores, mixer.cumulated
    lane = lax.broadcasted_iota(jnp.int32, (rows, LANES), 1)
    low = lane < HEAD_DIM

    def body(index, carry):
        d_scores, row_sums = carry
        where = block_at(index)
        d_ssd = k.d_ssd[:, where]
        value = k.inner[:, where]
        taps = tap_rows(k.inner_par, where)
        pre = conv_pre(row, value, taps, k.inner_par[4:5, where])
        pre_sig = jax.nn.sigmoid(pre)
        act = pre * pre_sig
        first = index * per_block
        rolled = pltpu.roll(cumulated, LANES - first, 1)
        d_inner = []
        for pair in range(per_block // 2):
            lanes = slice(pair * LANES, (pair + 1) * LANES)
            values = split_heads(act[:, lanes], low)
            d_pair = d_ssd[:, lanes]
            d_mix = matmul_nt(d_pair.astype(BF16), values)
            mixes = []
            for place in range(2):
                head, decay, step_row = decay_of(row, rolled, k, first, 2 * pair + place)
                part = d_mix[:, place * rows : (place + 1) * rows] * decay
                weighted = part * step_row
                d_scores = d_scores + weighted
                k.d_col[pl.ds(head, 1), :] = col_sum(part * scores)
                row_sum = jnp.sum(weighted * scores, axis=1, keepdims=True)
                row_sums = jnp.where(lane == head, row_sum, row_sums)
                mixes.append((scores * decay * step_row).astype(BF16))
            d_inner.append(matmul_tn(jnp.concatenate(mixes, axis=0), split_heads(d_pair, low)))
        d_act = jnp.concatenate(d_inner, axis=1) + k.inner_par[6:7, where] * d_ssd
        d_value, d_taps, d_bias = conv_back(row, d_act * silu_back(pre, pre_sig), value, taps)
        store_half(index, half_blocks, k.d_value_own, k.d_value_other, d_value.astype(BF16))
        if full:
            grads = jnp.concatenate(
                [*d_taps, d_bias, jnp.zeros_like(d_bias), col_sum(d_ssd * act), jnp.zeros_like(d_bias)],
                axis=0,
            )
            store_half(index, half_blocks, k.conv_own, k.conv_other, grads)
        return d_scores, row_sums

    zero = jnp.zeros((rows, LANES), F32)
    k.d_col[...] = jnp.zeros(k.d_col.shape, F32)
    d_scores, row_sums = lax.fori_loop(0, 2 * half_blocks, body, (zero, zero))
    k.d_scores[...] = d_scores
    k.row_sums[...] = row_sums


def input_back(row, k, load, full):
    inner, local, per_block, half_blocks = sizes(k)
    heads = local // HEAD_DIM
    mixer = mixer_inputs(row, k)
    d_col = k.d_col[...]
    d_cumulated = k.row_sums[...] - (d_col * mixer.step.T).T
    d_scaled = running_sum_back(row, d_cumulated)
    d_step = d_col.T + d_scaled * mixer.rate
    d_step_raw = d_step * jax.nn.sigmoid(mixer.step_in)
    d_step_q = d_step_raw.astype(BF16)
    d_scores_q = k.d_scores[...].astype(BF16)
    d_state_act = jnp.concatenate(
        [matmul_tn(d_scores_q, mixer.out_state), matmul(d_scores_q, mixer.in_state)], axis=1
    )
    d_state, d_taps, d_bias = conv_back(
        row, d_state_act * silu_back(mixer.pre, mixer.sig), mixer.state_pre, mixer.taps
    )
    d_state_q = d_state.astype(BF16)
    load.state.wait()
    load.own.wait()
    load.other.wait()
    residual, inverse_norm, _ = norm_parts(k)
    k.d_normed[...] = matmul_nt(d_step_q, k.w_step[...]) + matmul_nt(d_state_q, k.w_state[...])
    width = residual.shape[1]

    def project(index, carry):
        where = block_at(index)
        total = k.d_normed[:, where]
        aside = k.own_gate.shape[1] - local
        parts = (k.own_gate, k.d_value_own, k.core_gate, k.d_value_other)
        for number, part in enumerate(parts):
            span = slice(number * local, (number + 1) * local)
            part = part[...] if number % 2 else part[:, aside:]
            total = total + matmul_nt(part, k.w_in[where, span])
        k.d_normed[:, where] = total
        return carry

    lax.fori_loop(0, width // BLOCK, project, 0)
    d_normed = k.d_normed[...]
    scaled = d_normed * k.norm_par[...]
    mean = jnp.sum(scaled * residual, axis=1, keepdims=True) / width
    d_residual = inverse_norm * scaled - residual * (
        inverse_norm * inverse_norm * inverse_norm * mean
    )
    input_grad = k.grad_in[...].astype(F32) + d_residual
    k.grad[...] = input_grad.astype(k.grad.dtype)
    if not full:
        return
    half = d_state_q.shape[1] // 2
    is_first = k.ints[0, 0] == 0
    low_half, high_half = d_state[:, :half], d_state[:, half:]
    pairs = (
        (k.small_own, jnp.where(is_first, low_half, high_half), d_step_raw),
        (
            k.small_other,
            jnp.where(is_first, high_half, low_half),
            pltpu.roll(d_step_raw, LANES - heads, 1),
        ),
    )
    for target, state_part, step_part in pairs:
        target[...] = jnp.concatenate([state_part, step_part], axis=1).astype(BF16)
    bias_grad = col_sum(d_step_raw)
    decay_grad = col_sum(d_scaled * mixer.step) * mixer.rate
    lane = lax.broadcasted_iota(jnp.int32, bias_grad.shape, 1)
    norm_grad = col_sum(d_normed * residual * inverse_norm)
    state_row = jnp.concatenate(d_taps, axis=1)
    for number, (target, gain, conv) in enumerate(
        ((k.pack_own, k.gain_own, k.conv_own), (k.pack_other, k.gain_other, k.conv_other))
    ):
        target[...] = jnp.zeros(target.shape, F32)
        target[0:5, :] = conv[0:5, :]
        target[5:6, :] = gain[...]
        target[6:7, :] = conv[6:7, :]
        bias_part, decay_part = bias_grad, pltpu.roll(decay_grad, heads, 1)
        if number == 1:
            bias_part, decay_part = pltpu.roll(bias_grad, LANES - heads, 1), decay_grad
        head_row = jnp.where(lane < heads, bias_part, decay_part)
        target[7:8, 0:LANES] = head_row
        target[8:9, :] = norm_grad
        target[9:10, 0 : state_row.shape[1]] = state_row
        target[10:11, 0 : d_bias.shape[1]] = d_bias


class Load:
    def __init__(self):
        self.copies = []
        self.waited = False

    def start(self, source, target, sem):
        copy = pltpu.make_async_copy(source, target, sem)
        copy.start()
        self.copies.append(copy)

    def wait(self):
        if not self.waited:
            self.waited = True
            for copy in self.copies:
                copy.wait()


def start_loads(k, inward, outward, out_first):
    load = SimpleNamespace(state=Load(), own=Load(), other=Load(), out=Load())

    def start_out():
        rows = k.own_out.shape[0]
        load.out.start(k.own_out, k.w_out.at[pl.ds(0, rows), :], k.sems.at[0])
        load.out.start(k.other_out, k.w_out.at[pl.ds(rows, rows), :], k.sems.at[1])

    if outward and out_first:
        start_out()
    if inward:
        columns = k.own_in.shape[1]
        load.state.start(k.state_w, k.w_state, k.sems.at[2])
        load.state.start(k.step_w, k.w_step, k.sems.at[3])
        load.own.start(k.own_in, k.w_in.at[:, pl.ds(0, columns)], k.sems.at[4])
        load.other.start(k.other_in, k.w_in.at[:, pl.ds(columns, columns)], k.sems.at[5])
    if outward and not out_first:
        start_out()
    return load


def run_kernel(body, inputs, loaded, outputs, sent, scratch, flops, moved):
    loads = {name: (value.shape, value.dtype) for name, value in loaded.items()}
    names = [*inputs, *outputs, *scratch, *loads, *sent]
    vmem = pl.BlockSpec(memory_space=pltpu.VMEM)
    smem = pl.BlockSpec(memory_space=pltpu.SMEM)
    anywhere = pl.BlockSpec(memory_space=pl.ANY)

    def spec(value):
        if value.dtype == jnp.int32:
            return smem
        return anywhere if value.shape[0] >= 1024 else vmem

    def kernel(*refs):
        refs = list(refs)

        def take(count):
            taken = refs[:count]
            del refs[:count]
            return taken

        ins, sources = take(len(inputs)), take(len(loaded))
        outs, targets = take(len(outputs)), take(len(sent))
        k = SimpleNamespace(**dict(zip(names, ins + outs + take(len(names) - len(ins) - len(outs)))))
        k.sems = refs[0]
        number = 6
        ready, flush, waits = {}, {}, []
        for name, source in zip(loaded, sources):
            ready[name] = Load()
            ready[name].start(source, vars(k)[name], k.sems.at[number])
            number += 1
        for name, target in zip(sent, targets):
            flush[name] = pltpu.make_async_copy(vars(k)[name], target, k.sems.at[number])
            number += 1
        k.ready, k.flush = SimpleNamespace(**ready), SimpleNamespace(**flush)
        body(k)
        for copy in flush.values():
            copy.wait()

    results = pl.pallas_call(
        kernel,
        name=body.__name__,
        out_shape=[jax.ShapeDtypeStruct(*shape) for shape in (*outputs.values(), *sent.values())],
        in_specs=[spec(value) for value in inputs.values()] + [anywhere for _ in loaded],
        out_specs=[vmem for _ in outputs] + [anywhere for _ in sent],
        scratch_shapes=[
            pltpu.VMEM(*shape) for shape in (*scratch.values(), *loads.values(), *sent.values())
        ]
        + [pltpu.SemaphoreType.DMA((6 + len(loaded) + len(sent),))],
        compiler_params=pltpu.CompilerParams(vmem_limit_bytes=48 << 20),
        cost_estimate=pl.CostEstimate(flops=flops, bytes_accessed=moved, transcendentals=0),
    )(*inputs.values(), *loaded.values())
    return SimpleNamespace(**dict(zip([*outputs, *sent], results)))


def exchange(value, core_bit, dp_bit):
    count, cores = lax.axis_size("dp"), lax.axis_size("tensor")
    if dp_bit == 0:
        return lax.ppermute(value, "tensor", [(core, core ^ 1) for core in range(cores)])
    if core_bit == 0:
        return lax.ppermute(value, "dp", [(place, place ^ dp_bit) for place in range(count)])
    pairs = [
        (place * cores + core, (place ^ dp_bit) * cores + (core ^ 1))
        for place in range(count)
        for core in range(cores)
    ]
    return lax.ppermute(value, ("dp", "tensor"), pairs)


def swap_core(value):
    return exchange(value, 1, 0)


def swap_bit(value, bit):
    return exchange(value, 0, bit)


def near(own, to_core, to_x, to_both):
    return [own, exchange(to_core, 1, 0), exchange(to_x, 0, 1), exchange(to_both, 1, 1)]


def far(same, other, same_x, other_x):
    return [
        exchange(same, 0, 2),
        exchange(other, 1, 2),
        exchange(same_x, 0, 3),
        exchange(other_x, 1, 3),
    ]


def to_section(value, source, target):
    return lax.ppermute(value, "section", [(source, target)])


def in_order(own, other, first):
    return jnp.where(first, jnp.stack([own, other]), jnp.stack([other, own]))


def owner_offsets(count):
    bits = count.bit_length() - 1
    offsets = []
    for x_bit in range(2):
        for order in range(count // 2):
            place = x_bit
            for bit in range(1, bits):
                if (order >> (bits - 1 - bit)) & 1:
                    place |= 1 << bit
            offsets.append(place)
    return offsets


def arrange(k, source, place):
    share = source.shape[1] // (k.ints.shape[1] - 2)
    start = pl.multiple_of(k.ints[0, 2 + place] * share, share)
    return source[:, pl.ds(start, share)]


def arranged(values):
    count = lax.axis_size("dp")
    rows, width = values.shape
    owners = lax.axis_index("dp") ^ jnp.array(owner_offsets(count), jnp.int32)
    groups = jnp.take(values.reshape(rows, count, width // count), owners, axis=1)
    return groups.reshape(rows, width)


def product_pass(k):
    pieces = [k.left_0, k.left_1, k.left_2, k.left_3]
    rights = [k.right_0, k.right_1, k.right_2, k.right_3]
    rows = k.kept.shape[0]
    aside = k.right_0.shape[1] - k.kept.shape[1]
    left = jnp.concatenate([piece[:, : 2 * rows] for piece in pieces], axis=0)
    for start in range(0, k.kept.shape[1], BLOCK):
        where = slice(start, start + BLOCK)
        shifted = slice(start + aside, start + aside + BLOCK)
        right = jnp.concatenate([piece[:, shifted] for piece in rights], axis=0)
        total = matmul_tn(left, right)
        k.kept[:, where] = total[:rows]
        k.sent[:, where] = total[rows:].astype(BF16)


def product(lefts, rights, width, columns):
    inputs = dict(
        left_0=lefts[0],
        left_1=lefts[1],
        left_2=lefts[2],
        left_3=lefts[3],
        right_0=rights[0],
        right_1=rights[1],
        right_2=rights[2],
        right_3=rights[3],
    )
    rows = width // 4
    outputs = dict(kept=((rows, columns), F32), sent=((rows, columns), BF16))
    flops = 2 * 8 * rows * LANES * columns
    result = run_kernel(product_pass, inputs, {}, outputs, {}, {}, flops, 8 * rows * columns)
    return result.kept, result.sent


def halving(kept, sent, bit, axis):
    count = lax.axis_size("dp")
    total = kept + swap_bit(sent, bit).astype(F32)
    while 2 * bit < count:
        bit *= 2
        middle = total.shape[axis] // 2
        low = lax.slice_in_dim(total, 0, middle, axis=axis)
        high = lax.slice_in_dim(total, middle, 2 * middle, axis=axis)
        total = low + swap_bit(high.astype(BF16), bit).astype(F32)
    return total


def dp_total(value):
    bit = 1
    while bit < lax.axis_size("dp"):
        value = value + swap_bit(value, bit)
        bit *= 2
    return value


def local(
    block_input,
    seq_lengths,
    norm_gain,
    in_weight,
    state_weight,
    step_weight,
    conv_weight,
    conv_bias,
    state_conv,
    state_bias,
    step_bias,
    decay_log,
    skip_gain,
    gate_gain,
    out_weight,
    out_cotangent,
):
    core = lax.axis_index("tensor")
    count = lax.axis_size("dp")
    first_core = core == 0
    rows = block_input.shape[1]
    width, _, half = in_weight.shape[1:]
    inner = 2 * half
    heads = step_weight.shape[2]
    state = state_weight.shape[2]
    share = width // count
    inside = share % LANES == 0
    own_in = in_weight[0].reshape(width, inner)
    other_in = swap_core(own_in)
    own_out = out_weight[0]
    other_out = swap_core(own_out)
    own_step = step_weight[0]
    other_step = swap_core(own_step)
    own_par = jnp.concatenate(
        [
            conv_weight[0],
            conv_bias,
            gate_gain,
            jnp.repeat(skip_gain, HEAD_DIM, axis=1),
            jnp.concatenate(
                [step_bias, decay_log, jnp.zeros((1, half - 2 * heads), F32)], axis=1
            ),
        ],
        axis=0,
    )
    other_par = swap_core(own_par)

    def pad_lanes(value, lanes):
        return jnp.pad(value, ((0, 0), (0, lanes - value.shape[1])))

    def head_row(start):
        lanes = slice(start, start + heads)
        return pad_lanes(jnp.concatenate([own_par[7:8, lanes], other_par[7:8, lanes]], 1), LANES)

    owners = lax.axis_index("dp") ^ jnp.array(owner_offsets(count), jnp.int32)
    ints = dict(
        ints=jnp.concatenate(
            [jnp.stack([core, lax.axis_index("section")]).astype(jnp.int32), owners]
        )[None]
    )
    lengths = dict(lengths=lax.dynamic_slice_in_dim(seq_lengths[:, 0], core, 1, axis=0))
    norm_par = dict(norm_par=norm_gain)
    inner_par = dict(inner_par=jnp.concatenate([own_par, other_par], axis=1))
    mixer_par = dict(
        state_par=jnp.concatenate([state_conv[0], state_bias, jnp.zeros((3, state), F32)], axis=0),
        head_par=jnp.concatenate([head_row(0), head_row(heads), jnp.zeros((6, LANES), F32)], axis=0),
    )
    inward = dict(
        own_in=own_in,
        other_in=other_in,
        state_w=state_weight[0],
        step_w=pad_lanes(jnp.concatenate([own_step, other_step], axis=1), LANES),
    )
    outward = dict(own_out=own_out, other_out=other_out)
    inputs = dict(block_input=block_input)
    cotangents = dict(out_cotangent=out_cotangent)
    wide = (rows, width)
    inward_scratch = dict(
        w_in=((width, 2 * inner), BF16),
        w_state=((width, state), BF16),
        w_step=((width, LANES), BF16),
    )
    outward_scratch = dict(w_out=((inner, width), BF16))
    turned = dict(step_t=((LANES, rows), F32), cum_t=((LANES, rows), F32))
    row_input = dict(x=(wide, BF16))
    row_grad = dict(grad_in=(wide, BF16))
    kept_shapes = dict(
        gate=((rows, inner), F32),
        inner=((rows, inner), F32),
        ssd=((rows, inner), F32),
    )
    small_shapes = dict(
        state_pre=((rows, state), F32),
        step_raw=((rows, LANES), F32),
        inverse=((rows, LANES), F32),
    )
    normed_shapes = dict(normed=(wide, BF16))
    part = width // 2
    packs = dict(
        own_pack=((rows, part + half), BF16),
        core_pack=((rows, part + half), BF16),
        x_pack=((rows, part + half), BF16),
        both_pack=((rows, part + half), BF16),
    )
    gated_parts = dict(gated_own=((rows, half), BF16), gated_other=((rows, half), BF16))
    quarter = width // 4
    gate_two = dict(
        own_gate=((rows, quarter + half), BF16), core_gate=((rows, quarter + half), BF16)
    )
    gate_packs = dict(
        **gate_two,
        x_gate=((rows, quarter + half), BF16),
        both_gate=((rows, quarter + half), BF16),
        far_grad=((rows, quarter), BF16),
        far_grad_x=((rows, quarter), BF16),
    )
    d_ssd_shape = dict(d_ssd=((rows, inner), F32))
    values_two = dict(d_value_own=((rows, half), BF16), d_value_other=((rows, half), BF16))
    mix_small = dict(
        d_col=((LANES, rows), F32),
        d_scores=((rows, rows), F32),
        row_sums=((rows, LANES), F32),
    )
    gains = dict(gain_own=((1, half), F32), gain_other=((1, half), F32))
    convs = dict(conv_own=((8, half), F32), conv_other=((8, half), F32))
    normed_grad = dict(d_normed=(wide, F32))
    result = dict(result=(wide, BF16))
    work = 2 * rows * width * inner
    weight_bytes = 2 * width * inner

    def choose_input(k):
        chosen = k.block_input[k.ints[0, 0]]
        first = jnp.broadcast_to(k.ints[0, 1], chosen.shape) == 0
        k.x[...] = jnp.where(first, chosen.astype(F32), k.carried[...].astype(F32)).astype(BF16)

    def choose_grad(k):
        chosen = k.out_cotangent[k.ints[0, 0]]
        first = jnp.broadcast_to(k.ints[0, 1], chosen.shape) == 0
        received = k.grad_carried[...].astype(F32)
        k.grad_in[...] = jnp.where(first, received, chosen.astype(F32)).astype(BF16)

    def forward_pass(k):
        load = start_loads(k, True, True, False)
        k.x[...] = k.block_input[k.ints[0, 0]]
        forward(Row(k.lengths, rows), k, load)
        k.flush.result.start()

    def both_passes(k):
        load = start_loads(k, True, True, False)
        row = Row(k.lengths, rows)
        choose_input(k)
        k.grad_in[...] = k.out_cotangent[k.ints[0, 0]]
        forward(row, k, load)
        k.flush.gate.start()
        k.flush.inner.start()
        k.flush.ssd.start()
        k.flush.result.start()
        for place in range(count):
            first, second = (k.own_pack, k.core_pack) if 2 * place < count else (k.x_pack, k.both_pack)
            if inside:
                where = slice(place * share, (place + 1) * share)
                if 2 * place >= count:
                    where = slice(place * share - part, (place + 1) * share - part)
                first[:, where] = arrange(k, k.normed, place)
                second[:, where] = first[:, where]
            elif place % (count // 2) == 0:
                first[:, :part] = jnp.zeros((rows, part), BF16)
                second[:, :part] = jnp.zeros((rows, part), BF16)
        k.gated_own[...] = k.own_pack[:, part:]
        k.gated_other[...] = k.core_pack[:, part:]
        k.x_pack[:, part:] = k.own_pack[:, part:]
        k.both_pack[:, part:] = k.core_pack[:, part:]
        k.flush.own_pack.start()
        k.flush.core_pack.start()
        k.flush.x_pack.start()
        k.flush.both_pack.start()
        k.flush.gated_own.start()
        k.flush.gated_other.start()
        gate_back(row, k, load, False)
        mix_back(row, k, False)
        input_back(row, k, load, False)
        k.flush.grad.start()

    def gate_pass(k):
        load = start_loads(k, False, True, True)
        choose_grad(k)
        for place in range(count):
            wanted = place * share % quarter
            where = slice(wanted, wanted + share)
            targets = (
                (k.own_gate, k.core_gate),
                (k.far_grad,),
                (k.x_gate, k.both_gate),
                (k.far_grad_x,),
            )[place * share // quarter]
            for target in targets:
                if inside:
                    target[:, where] = arrange(k, k.grad_in, place)
                elif wanted == 0:
                    target[:, :quarter] = jnp.zeros((rows, quarter), BF16)
        k.flush.far_grad.start()
        k.flush.far_grad_x.start()
        k.ready.gate.wait()
        k.ready.ssd.wait()
        gate_back(SimpleNamespace(rows=rows), k, load, True)
        k.x_gate[:, quarter:] = k.own_gate[:, quarter:]
        k.both_gate[:, quarter:] = k.core_gate[:, quarter:]
        k.flush.own_gate.start()
        k.flush.core_gate.start()
        k.flush.x_gate.start()
        k.flush.both_gate.start()
        k.flush.d_ssd.start()

    def mix_pass(k):
        row = Row(k.lengths, rows)
        k.ready.inner.wait()
        k.ready.d_ssd.wait()
        mix_back(row, k, True)
        k.flush.d_value_own.start()
        k.flush.d_value_other.start()

    def input_pass(k):
        load = start_loads(k, True, False, False)
        choose_input(k)
        choose_grad(k)
        input_back(Row(k.lengths, rows), k, load, True)
        k.flush.grad.start()

    def out_pass(k):
        grads = [k.grad_0, k.grad_1, k.grad_2, k.grad_3]
        grads = [piece[:, :quarter] for piece in grads]
        grads += [k.far_0[...], k.far_1[...], k.far_2[...], k.far_3[...]]
        right = jnp.concatenate(grads, axis=0)
        keep = quarter // 2
        for start in range(0, half, BLOCK):
            where = slice(start, start + BLOCK)
            shifted = slice(start + part, start + part + BLOCK)
            pieces = [piece[:, shifted] for piece in (k.pack_0, k.pack_1, k.pack_2, k.pack_3)]
            pieces += [piece[:, where] for piece in (k.gated_0, k.gated_1, k.gated_2, k.gated_3)]
            total = matmul_tn(jnp.concatenate(pieces, axis=0), right)
            k.kept[where, :] = total[:, :keep]
            k.sent[where, :] = total[:, keep:].astype(BF16)

    shared = {**ints, **lengths, **norm_par, **inner_par, **mixer_par, **inward, **outward}
    weights = {**inward_scratch, **outward_scratch}

    middle = run_kernel(
        forward_pass,
        {**inputs, **shared},
        {},
        {},
        result,
        {
            **row_input,
            **kept_shapes,
            **small_shapes,
            **normed_shapes,
            **packs,
            **turned,
            **weights,
        },
        3 * work,
        3 * weight_bytes,
    )
    carried = dict(carried=to_section(middle.result, 0, 1))
    keep = run_kernel(
        both_passes,
        {**inputs, **carried, **cotangents, **shared},
        {},
        small_shapes,
        {**dict(grad=(wide, BF16)), **result, **kept_shapes, **packs, **gated_parts},
        {
            **row_input,
            **row_grad,
            **normed_shapes,
            **turned,
            **d_ssd_shape,
            **gate_two,
            **values_two,
            **mix_small,
            **normed_grad,
            **weights,
        },
        6 * work,
        3 * weight_bytes,
    )
    grad_carried = dict(grad_carried=to_section(keep.grad, 1, 0))

    def with_left(columns, packed):
        return jnp.concatenate([columns, packed[:, columns.shape[1] :]], axis=1)

    packed = [keep.own_pack, keep.core_pack, keep.x_pack, keep.both_pack]
    if not inside:
        hidden = jnp.where(
            lax.axis_index("section") == 0,
            lax.dynamic_index_in_dim(block_input, core, 0, keepdims=False),
            carried["carried"],
        ).astype(F32)
        mean = jnp.mean(hidden * hidden, axis=1, keepdims=True)
        normed = arranged((hidden * lax.rsqrt(mean + EPS) * norm_gain).astype(BF16))
        lefts = (normed[:, :part], normed[:, :part], normed[:, part:], normed[:, part:])
        packed = [with_left(*pair) for pair in zip(lefts, packed)]
    pieces = near(*packed)
    far_gated = far(keep.gated_own, keep.gated_other, keep.gated_own, keep.gated_other)

    gated = run_kernel(
        gate_pass,
        {
            **grad_carried,
            **cotangents,
            **ints,
            **inner_par,
            **outward,
            **dict(inverse=keep.inverse),
        },
        dict(gate=keep.gate, ssd=keep.ssd),
        gains,
        {**gate_packs, **d_ssd_shape},
        {**row_grad, **outward_scratch},
        work,
        weight_bytes,
    )
    gate_packed = [gated.own_gate, gated.core_gate, gated.x_gate, gated.both_gate]
    far_sent = [gated.far_grad, gated.far_grad, gated.far_grad_x, gated.far_grad_x]
    if not inside:
        grad_in = arranged(
            jnp.where(
                lax.axis_index("section") == 0,
                grad_carried["grad_carried"],
                lax.dynamic_index_in_dim(out_cotangent, core, 0, keepdims=False),
            )
        )
        quarters = jnp.split(grad_in, 4, axis=1)
        lefts = (quarters[0], quarters[0], quarters[2], quarters[2])
        gate_packed = [with_left(*pair) for pair in zip(lefts, gate_packed)]
        far_sent = [quarters[1], quarters[1], quarters[3], quarters[3]]
    gate_pieces = near(*gate_packed)
    far_grads = far(*far_sent)

    mixer_kept = dict(state_pre=keep.state_pre, step_raw=keep.step_raw)
    mixed = run_kernel(
        mix_pass,
        {**lengths, **inner_par, **mixer_par, **mixer_kept},
        dict(inner=keep.inner, d_ssd=gated.d_ssd),
        {**mix_small, **convs},
        values_two,
        turned,
        work,
        weight_bytes,
    )
    value_pieces = near(
        mixed.d_value_own, mixed.d_value_other, mixed.d_value_own, mixed.d_value_other
    )
    back = run_kernel(
        input_pass,
        {
            **inputs,
            **carried,
            **cotangents,
            **grad_carried,
            **ints,
            **lengths,
            **norm_par,
            **inner_par,
            **mixer_par,
            **mixer_kept,
            **inward,
            **dict(own_gate=gated.own_gate, core_gate=gated.core_gate),
            **dict(gain_own=gated.gain_own, gain_other=gated.gain_other),
            **vars(mixed),
        },
        {},
        dict(
            small_own=((rows, 2 * LANES), BF16),
            small_other=((rows, 2 * LANES), BF16),
            pack_own=((16, half), F32),
            pack_other=((16, half), F32),
        ),
        dict(grad=(wide, F32)),
        {**row_input, **row_grad, **normed_grad, **inward_scratch},
        2 * work,
        2 * weight_bytes,
    )
    out_parts = run_kernel(
        out_pass,
        dict(
            pack_0=pieces[0],
            pack_1=pieces[1],
            pack_2=pieces[2],
            pack_3=pieces[3],
            gated_0=far_gated[0],
            gated_1=far_gated[1],
            gated_2=far_gated[2],
            gated_3=far_gated[3],
            grad_0=gate_pieces[0],
            grad_1=gate_pieces[1],
            grad_2=gate_pieces[2],
            grad_3=gate_pieces[3],
            far_0=far_grads[0],
            far_1=far_grads[1],
            far_2=far_grads[2],
            far_3=far_grads[3],
        ),
        {},
        dict(kept=((half, quarter // 2), F32), sent=((half, quarter // 2), BF16)),
        {},
        {},
        work,
        weight_bytes,
    )
    out_sum = halving(out_parts.kept, out_parts.sent, 4, 1)
    gate_sum = halving(*product(pieces, gate_pieces, width, half), 2, 0)
    value_sum = halving(*product(pieces, value_pieces, width, half), 2, 0)
    small_pieces = near(back.small_own, back.small_other, back.small_own, back.small_other)
    small_sum = halving(*product(pieces, small_pieces, width, 2 * LANES), 2, 0)
    section_output = in_order(keep.result, swap_core(keep.result), first_core)
    input_grad = in_order(back.grad, swap_core(back.grad), first_core)
    small = dp_total(back.pack_own + swap_core(back.pack_other))

    own_state = small_sum[:, : state // 2]
    other_state = swap_core(own_state)
    state_sum = jnp.where(
        first_core,
        jnp.concatenate([own_state, other_state], axis=1),
        jnp.concatenate([other_state, own_state], axis=1),
    )
    return (
        section_output[None],
        input_grad[None],
        lax.dynamic_slice_in_dim(small[8:9], lax.axis_index("dp") * share, share, 1),
        jnp.stack([gate_sum, value_sum], axis=1)[None],
        state_sum[None],
        small_sum[:, state // 2 : state // 2 + heads][None],
        small[0:4][None],
        small[4:5],
        small[9, : 4 * state].reshape(1, 4, state),
        small[10:11, :state],
        small[7:8, :heads],
        small[7:8, heads : 2 * heads],
        jnp.sum(small[6].reshape(1, heads, HEAD_DIM), axis=2),
        small[5:6],
        out_sum[None],
    )


def solution(mesh):
    per_row = P(None, "dp", None)
    by_section = P("section", None)
    by_core = P("section", "tensor")
    columns = P("section", None, "tensor")
    whole = P("section", None, None)
    rows_out = P("section", None, "dp", None)
    return jax.shard_map(
        local,
        mesh=mesh,
        in_specs=(
            per_row,
            per_row,
            by_section,
            P("section", None, None, "tensor"),
            whole,
            columns,
            columns,
            by_core,
            whole,
            by_section,
            by_core,
            by_core,
            by_core,
            by_core,
            P("section", "tensor", None),
            per_row,
        ),
        out_specs=(
            rows_out,
            rows_out,
            P("section", "dp"),
            P("section", "dp", None, "tensor"),
            P("section", "dp", None),
            P("section", "dp", "tensor"),
            columns,
            by_core,
            whole,
            by_section,
            by_core,
            by_core,
            by_core,
            by_core,
            P("section", "tensor", "dp"),
        ),
        check_vma=False,
    )
```
